256 devices in a mesh: net: 16 (over z, x_hi), mem: 16 (over x_lo, y, core).
Axes of the slice: x: 4 (x_hi: 2, x_lo: 2; x = x_hi * 2 + x_lo), y: 4, z: 8, core: 2. Of those that a mesh axis runs over, the one named last changes fastest.
Arguments:
- stored_reach_flows: bfloat16 [5, 512, 65536], P(None, 'mem', 'net'), may hold values from 0.19921875 to 5
- lateral: bfloat16 [4, 512, 65536], P(None, 'mem', 'net'), may hold values from 0.049804688 to 1
- cotangent: bfloat16 [4, 512, 65536], P(None, 'mem', 'net'), may hold values from -3 to 3
- roughness: float32 [65536], P('net'), may hold values from 0.02 to 0.1
- travel_factor: float32 [65536], P('net'), may hold values from 0.2 to 5
- inverse_block_matrix: float32 [512, 128, 128], P('net'), may hold values from 0 to 1, as said below
- down_in_block: int32 [65536], P('net'), may hold values from 1 to 128, as said below
- exit_slot: int32 [65536], P('net'), may hold values from -1 to 127, as said below
- inlet_reach: int32 [16, 128], P('net'), may hold values from 1 to 3999, as said below
Outputs:
- grad_lateral: bfloat16 [4, 512, 65536], P(None, 'mem', 'net')
- grad_rough: float32 [65536], P(('net', 'mem'))
The draws below stay inside these ranges and needn't reach their ends.
Inputs may be any that keep to these rules, and one draw needn't show every extreme that they name: Within a block a reach feeds a later position: down_in_block[r] > r % 128 where it is under 128. exit_slot[r] >= 0 only where down_in_block[r] == 128 and r is not in the last partition; every reach of the last partition has -1. `inlet_reach`: each entry is a reach at positions 1 to 31 of some block of that partition; several slots may name the same reach. inverse_block_matrix[k][i, j] is 1 where i = j, the product of weight_new over the reaches after j up to and including i where i lies on the in-block path of next reaches from j, and 0 elsewhere.
All inputs are finite; a program needn't handle non-finite values.
Results may differ from the reference program's by a relative error of at most 0.001.
Values sent between devices are 32-bit elements; how exact they have to be, the bound alone decides.
A program may use at most 64 MiB of HBM per device.

```python
import math
import jax
import jax.numpy as jnp
from jax import lax

NBLK = 32
NIN = 128
STEPS = 4
R_DEV = 4096
REACHES = 65536
MEMBERS = 512
N_NET = 16


def link_layout(key):
    link_key = jax.random.fold_in(key, 11)
    slot_key = jax.random.fold_in(key, 12)
    head_key = jax.random.fold_in(key, 13)
    partitions = REACHES // R_DEV
    slot_ids = jnp.arange(NIN, dtype=jnp.int32)[None, :]
    head_pos = jax.random.randint(head_key, (partitions, NIN), 1, 32, dtype=jnp.int32)
    head_pos = jnp.where(slot_ids == NIN - 1, 31, jnp.where(slot_ids == 0, 1, head_pos))
    inlets = (slot_ids % NBLK * 128 + head_pos).astype(jnp.int32)
    reach_ids = jnp.arange(REACHES, dtype=jnp.int32)
    position = reach_ids % 128
    stride = jax.random.randint(jax.random.fold_in(link_key, 1), (REACHES,), 1, 9, dtype=jnp.int32)
    retained_values = jax.random.randint(jax.random.fold_in(link_key, 2), (REACHES,), 0, 100, dtype=jnp.int32)
    target = position + stride
    down_pos = jnp.where((retained_values < 85) & (target <= 127), target, 128)
    inlet_global = (jnp.arange(partitions, dtype=jnp.int32)[:, None] * R_DEV + inlets).reshape(-1)
    marked = jnp.zeros((REACHES,), dtype=bool).at[inlet_global].set(True)
    down_pos = jnp.where(marked, 128, down_pos)
    down_pos = jnp.where(reach_ids == 0, 1, down_pos).astype(jnp.int32)
    partition = reach_ids // R_DEV
    slot_pick = jax.random.randint(slot_key, (REACHES,), 0, NIN, dtype=jnp.int32)
    slot_pick = jnp.where(reach_ids % R_DEV == 127, NIN - 1, slot_pick)
    boundary = (down_pos == 128) & (partition < partitions - 1)
    exit_ids = jnp.where(boundary, slot_pick, -1).astype(jnp.int32)
    return (down_pos, exit_ids, inlets, marked)


def coefficient_draws(key):
    rough_key = jax.random.fold_in(key, 21)
    factor_key = jax.random.fold_in(key, 22)
    marked = link_layout(key)[3]
    roughness_uniform = jax.random.uniform(rough_key, (REACHES,), jnp.float32)
    travel_factor_uniform = jax.random.uniform(factor_key, (REACHES,), jnp.float32)
    roughness_draw = jnp.exp(jnp.log(0.02) + roughness_uniform * (jnp.log(0.1) - jnp.log(0.02)))
    fast_factor = jnp.exp(jnp.log(0.2) + travel_factor_uniform * (jnp.log(0.5) - jnp.log(0.2)))
    slow_factor = jnp.exp(jnp.log(0.5) + travel_factor_uniform * (jnp.log(5.0) - jnp.log(0.5)))
    roughness_draw = jnp.clip(roughness_draw, 0.02, 0.1).astype(jnp.float32)
    factor_draw = jnp.clip(jnp.where(marked, fast_factor, slow_factor), 0.2, 5.0).astype(jnp.float32)
    return (roughness_draw, factor_draw)


def draw_roughness(key, part):
    return coefficient_draws(key)[0]


def draw_travel_factor(key, part):
    return coefficient_draws(key)[1]


def draw_down_in_block(key, part):
    return link_layout(key)[0]


def draw_exit_slot(key, part):
    return link_layout(key)[1]


def draw_inlet_reach(key, part):
    return link_layout(key)[2]


def draw_inverse_block_matrix(key, part):
    down_pos = link_layout(key)[0]
    roughness_draw, factor_draw = coefficient_draws(key)
    travel = roughness_draw * factor_draw
    divisor = 0.8 * travel + 0.5
    weight_new = (0.5 - 0.2 * travel) / divisor
    block_count = REACHES // 128
    down_blocks = down_pos.reshape(block_count, 128)
    weight_blocks = weight_new.reshape(block_count, 128)
    row_ids = jnp.arange(128, dtype=jnp.int32)

    def column_step(counter, matrix):
        position = 127 - counter
        target = lax.dynamic_index_in_dim(down_blocks, position, 1, False)
        interior_reaches = target < 128
        clipped = jnp.minimum(target, 127).astype(jnp.int32)
        path_gain = jnp.take_along_axis(weight_blocks, clipped[:, None], axis=1)[:, 0]
        path_gain = jnp.where(interior_reaches, path_gain, 0.0)
        index_grid = jnp.broadcast_to(clipped[:, None, None], (block_count, 128, 1))
        downstream = jnp.take_along_axis(matrix, index_grid, axis=2)
        unit_column = jnp.where(row_ids == position, 1.0, 0.0).astype(jnp.float32)[None, :, None]
        column_new = unit_column + path_gain[:, None, None] * downstream
        return lax.dynamic_update_slice_in_dim(matrix, column_new.astype(jnp.float32), position, axis=2)
    start_matrix = jnp.zeros((block_count, 128, 128), jnp.float32)
    return lax.fori_loop(0, 128, column_step, start_matrix).astype(jnp.float32)


def block_scale(rng, shape, pieces, least, high):
    loudness = 1.0
    for dim, blocks in pieces:
        heights = jax.random.uniform(jax.random.fold_in(jax.random.fold_in(rng, 6), dim), (blocks,), jnp.float32, least / len(pieces), high / len(pieces))
        loudness = loudness * jnp.repeat(jnp.exp(heights), shape[dim] // blocks).reshape((-1,) + (1,) * (len(shape) - 1 - dim))
    return loudness


def gaussian(stream_key, extent, spread, most, shards=(), kind=jnp.bfloat16):
    array = jax.random.normal(stream_key, extent, jnp.float32) * spread
    if len(shards) > 0:
        array = block_scale(stream_key, extent, shards, -0.22, 0.18) * array
    return jnp.clip(array, min=-most, max=most).astype(kind)


def setup_inputs(seed: int = 0) -> dict:
    key_list = jax.random.split(jax.random.key(seed), 10)
    stored_reach_flows = jnp.clip(jnp.exp(math.log(5.0) - 3.2227897 * jax.random.uniform(key_list[0], (STEPS + 1, MEMBERS, REACHES), jnp.float32) ** block_scale(key_list[0], (STEPS + 1, MEMBERS, REACHES), ((1, 16), (2, 16)), -0.2, 0.2)), 0.19921875, 5.0).astype(jnp.bfloat16)
    lateral = jnp.clip(jnp.exp(math.log(1.0) - 2.9996462 * jax.random.uniform(key_list[1], (STEPS, MEMBERS, REACHES), jnp.float32) ** block_scale(key_list[1], (STEPS, MEMBERS, REACHES), ((1, 16), (2, 16)), -0.2, 0.2)), 0.049804688, 1.0).astype(jnp.bfloat16)
    cotangent = gaussian(key_list[2], (STEPS, MEMBERS, REACHES), 0.5, 3.0, ((1, 16), (2, 16)))
    roughness = draw_roughness(jax.random.fold_in(key_list[9], 71), 0)
    travel_factor = draw_travel_factor(jax.random.fold_in(key_list[9], 71), 0)
    inverse_block_matrix = draw_inverse_block_matrix(jax.random.fold_in(key_list[9], 71), 0)
    down_in_block = draw_down_in_block(jax.random.fold_in(key_list[9], 71), 0)
    exit_slot = draw_exit_slot(jax.random.fold_in(key_list[9], 71), 0)
    inlet_reach = draw_inlet_reach(jax.random.fold_in(key_list[9], 71), 0)
    return dict(stored_reach_flows=stored_reach_flows, lateral=lateral, cotangent=cotangent, roughness=roughness, travel_factor=travel_factor, inverse_block_matrix=inverse_block_matrix, down_in_block=down_in_block, exit_slot=exit_slot, inlet_reach=inlet_reach)


skew_weight = 0.2


def coefficients(roughness, travel_factor):
    travel = roughness * travel_factor
    divisor = travel * (1.0 - skew_weight) + 0.5
    weight_new = (0.5 - travel * skew_weight) / divisor
    weight_old = (0.5 + travel * skew_weight) / divisor
    weight_stay = (travel * (1.0 - skew_weight) - 0.5) / divisor
    weight_side = 1.0 / divisor
    square = divisor * divisor
    updated_slope = -0.5 / square
    slope_old = (skew_weight - 0.5) / square
    slope_stay = (1.0 - skew_weight) / square
    slope_side = (skew_weight - 1.0) / square
    return (weight_new, weight_old, weight_stay, weight_side), (updated_slope, slope_old, slope_stay, slope_side)


def reference(stored_reach_flows, lateral, cotangent, roughness, travel_factor, inverse_block_matrix, down_in_block, exit_slot, inlet_reach):
    weights, slopes = coefficients(roughness, travel_factor)
    weight_new, weight_old, weight_stay, weight_side = weights
    updated_slope, slope_old, slope_stay, slope_side = slopes
    reach_ids = jnp.arange(REACHES, dtype=jnp.int32)
    part_ids = reach_ids // R_DEV
    block_start = (reach_ids // 128) * 128
    next_part = jnp.minimum(part_ids + 1, N_NET - 1)
    inlet_global = next_part * R_DEV + inlet_reach[next_part, jnp.maximum(exit_slot, 0)]
    down_reach = jnp.where(down_in_block < 128, block_start + down_in_block,
                           jnp.where(exit_slot >= 0, inlet_global, REACHES)).astype(jnp.int32)
    crossing = exit_slot >= 0

    def inflow_of(current_instant):
        flow_level = stored_reach_flows[current_instant].astype(jnp.float32)
        summed = jax.ops.segment_sum(flow_level.T, down_reach, num_segments=REACHES + 1)
        return summed[:REACHES].T

    adjoint_next = jnp.zeros((MEMBERS, REACHES), jnp.float32)
    grad_total = jnp.zeros((REACHES,), jnp.float32)
    lateral_grads = [None] * STEPS
    for counter in range(STEPS):
        current_instant = STEPS - counter
        padded = jnp.concatenate([weight_old * adjoint_next, jnp.zeros((MEMBERS, 1), jnp.float32)], axis=1)
        pulled = jnp.take(padded, down_reach, axis=1)
        source = cotangent[current_instant - 1].astype(jnp.float32) + weight_stay * adjoint_next + pulled
        adjoint_parts = [None] * N_NET
        for partition in reversed(range(N_NET)):
            offset = partition * R_DEV
            right_side = source[:, offset:offset + R_DEV]
            if partition + 1 < N_NET:
                weighted_down = adjoint_parts[partition + 1] * weight_new[offset + R_DEV:offset + 2 * R_DEV]
                local_index = inlet_reach[partition + 1][jnp.maximum(exit_slot[offset:offset + R_DEV], 0)]
                external = jnp.where(crossing[offset:offset + R_DEV][None, :],
                                     jnp.take(weighted_down, local_index, axis=1), 0.0)
                right_side = right_side + external
            reshaped_values = right_side.reshape(MEMBERS, NBLK, 128)
            inverse_portion = inverse_block_matrix[partition * NBLK:(partition + 1) * NBLK]
            solved_adjoint = jnp.einsum("acj,cjv->acv", reshaped_values, inverse_portion, precision=lax.Precision.HIGHEST)
            adjoint_parts[partition] = solved_adjoint.reshape(MEMBERS, R_DEV)
        adjoint = jnp.concatenate(adjoint_parts, axis=1)
        factor = (updated_slope * inflow_of(current_instant) + slope_old * inflow_of(current_instant - 1)
                  + slope_stay * stored_reach_flows[current_instant - 1].astype(jnp.float32)
                  + slope_side * lateral[current_instant - 1].astype(jnp.float32))
        grad_total = grad_total + jnp.sum(adjoint * factor, axis=0)
        lateral_grads[current_instant - 1] = (weight_side * adjoint).astype(jnp.bfloat16)
        adjoint_next = adjoint
    return jnp.stack(lateral_grads), travel_factor * grad_total
```

```python
import jax
import jax.numpy as jnp
from jax import lax
from jax.experimental import pallas as pl
from jax.experimental.pallas import tpu as pltpu
from jax.sharding import PartitionSpec as P

F32, BF16 = jnp.float32, jnp.bfloat16
LANES = 128
GROUP = 8
MESH = pl.DeviceIdType.MESH


def dot(a, b):
    return lax.dot_general(a, b, (((1,), (0,)), ((), ())), preferred_element_type=F32)


def dot_t(a, b):
    return lax.dot_general(a, b, (((1,), (1,)), ((), ())), preferred_element_type=F32)


def split(value):
    high = value.astype(BF16)
    return high, (value - high.astype(F32)).astype(BF16)


def rows_of(rows, count=8):
    place = lax.broadcasted_iota(jnp.int32, (count, LANES), 0)
    out = jnp.zeros((count, LANES), F32)
    for i, row in enumerate(rows):
        out = jnp.where(place == i, jnp.broadcast_to(row, (count, LANES)), out)
    return out


def one_hot(row, start):
    place = lax.broadcasted_iota(jnp.int32, (LANES, LANES), 0) + start
    return jnp.where(place == row, 1.0, 0.0).astype(BF16)


def local_kernel(
    cot_ref, flow_ref, rough_ref, factor_ref, exit_ref, matrix_ref, inlet_ref,
    local_ref, gain_ref, inner_ref, leaving_ref,
):
    step = pl.program_id(0)
    steps, members = cot_ref.shape[0], cot_ref.shape[1]
    inlet = inlet_ref[...]
    inner = jnp.zeros((2 * (steps * members + 8), LANES), F32)
    leaving = jnp.zeros(leaving_ref.shape, F32)
    for j in range(GROUP):
        lanes = slice(j * LANES, (j + 1) * LANES)
        travel = rough_ref[j : j + 1, :] * factor_ref[j : j + 1, :]
        divisor = 0.8 * travel + 0.5
        numer_new = 0.5 - 0.2 * travel
        numer_old = 0.5 + 0.2 * travel
        weight_new = numer_new / divisor
        weight_old = numer_old / divisor
        ratio = numer_old / numer_new
        carry = (0.8 * travel - 0.5) / divisor + ratio
        exits = exit_ref[j : j + 1, :]
        matrix = matrix_ref[j]
        high, low = split(matrix)
        pattern = jnp.where(matrix != 0.0, 1.0, 0.0).astype(BF16)
        opened = jnp.where(exits >= 0, 1.0, 0.0)
        numbered = rows_of([jnp.where(exits >= 0, exits + 1, 0).astype(F32)])
        slot = dot(numbered.astype(BF16), pattern)[0:1]
        adjoint = None
        found = [None] * steps
        gains = []
        for t in reversed(range(steps)):
            start = cot_ref[t, :, lanes].astype(F32)
            if adjoint is None:
                x = jnp.concatenate([start, rows_of([opened])], 0).astype(BF16)
                adjoint = dot(x, high) + dot(x, low)
            else:
                x = jnp.concatenate([start, jnp.zeros((8, LANES), F32)], 0) + adjoint * carry
                x_high, x_low = split(x)
                adjoint = dot(x_high, high) + dot(x_low, high) + dot(x_high, low) - adjoint * ratio
            found[t] = adjoint[:members]
            local_ref[t, :, lanes] = adjoint[:members]
            gains.append(adjoint[members : members + 1])
        facts = rows_of(gains + [slot, weight_new, weight_old])
        gain_ref[:, lanes] = facts
        stacked = jnp.concatenate(found + [facts], 0)
        stacked_high = stacked.astype(BF16).astype(F32)
        both = jnp.concatenate([stacked_high, stacked - stacked_high], 0).astype(BF16)
        inner = inner + dot(both, one_hot(inlet, (step * GROUP + j) * LANES))
        flow = flow_ref[:, :, lanes].reshape(leaving_ref.shape)
        leaving = leaving + dot_t(flow, one_hot(exits, 0))
    rows = inner.shape[0] // 2
    inner = inner[:rows] + inner[rows:]

    @pl.when(step == 0)
    def _():
        inner_ref[...] = inner
        leaving_ref[...] = leaving

    @pl.when(step > 0)
    def _():
        inner_ref[...] += inner
        leaving_ref[...] += leaving


def exchange_kernel(
    inner_ref, leaving_ref, outer_ref, own_ref, arrived_ref,
    out_box, in_box, back_box, home_box, send, recv, back_send, back_recv, flow_sem,
):
    count = out_box.shape[0]
    me = lax.axis_index("net")
    barrier = pltpu.get_barrier_semaphore()
    for i in range(1, count):
        peer = lax.rem(me + i, count)
        pl.semaphore_signal(barrier, inc=1, device_id={"net": peer}, device_id_type=MESH)
    rows = inner_ref.shape[0] - 8
    for k in range(count):
        out_box[k, 0:8, :] = inner_ref[pl.ds(k, 8, stride=rows // 8), :]
        out_box[k, 8:16, :] = inner_ref[rows : rows + 8, :]
    in_box[me] = out_box[me]
    pl.semaphore_wait(barrier, count - 1)

    def outward(peer, slot):
        return pltpu.make_async_remote_copy(
            src_ref=out_box.at[peer], dst_ref=in_box.at[slot], send_sem=send.at[peer], recv_sem=recv.at[slot],
            device_id={"net": peer}, device_id_type=MESH,
        )

    def homeward(peer, slot):
        return pltpu.make_async_remote_copy(
            src_ref=back_box.at[peer], dst_ref=home_box.at[slot], send_sem=back_send.at[peer],
            recv_sem=back_recv.at[slot], device_id={"net": peer}, device_id_type=MESH,
        )

    def flows(peer):
        return pltpu.make_async_remote_copy(
            src_ref=leaving_ref, dst_ref=arrived_ref, send_sem=flow_sem.at[0], recv_sem=flow_sem.at[1],
            device_id={"net": peer}, device_id_type=MESH,
        )

    for i in range(1, count):
        outward(lax.rem(me + i, count), me).start()

    @pl.when(me < count - 1)
    def _():
        flows(me + 1).start()

    place = lax.broadcasted_iota(jnp.int32, (8, LANES), 0)
    number = lax.broadcasted_iota(jnp.int32, (LANES, LANES), 0).astype(F32) + 1.0
    outer = jnp.zeros((8, LANES), F32)
    for p in reversed(range(count)):

        @pl.when(me != p)
        def _():
            outward(p, p).wait_recv()

        own = in_box[p, 0:8, :]
        if p < count - 1:
            picked = jnp.where(number == in_box[p, 12:13, :], 1.0, 0.0).astype(BF16)
            outer_high = outer.astype(BF16).astype(F32)
            both = jnp.concatenate([outer_high, outer - outer_high], 0).astype(BF16)
            both = dot(both, picked)
            taken = both[:8] + both[8:]
            own = own + taken * in_box[p, 8:9, :]
            for d in range(1, 4):
                later = jnp.where(place < 8 - 2 * d, pltpu.roll(taken, 8 - 2 * d, 0), 0.0)
                own = own + later * in_box[p, 8 + d : 9 + d, :]
        back_box[p, 0:8, :] = outer
        back_box[p, 8:16, :] = own

        @pl.when(me != p)
        def _():
            homeward(p, me).start()

        @pl.when(me == p)
        def _():
            home_box[p] = back_box[p]

        outer = own * in_box[p, 13:14, :] + jnp.where(place < 6, pltpu.roll(own, 6, 0), 0.0) * in_box[p, 14:15, :]

    for k in range(count):

        @pl.when(me != k)
        def _():
            homeward(k, k).wait_recv()

        outer_ref[pl.ds(k, 8, stride=rows // 8), :] = home_box[k, 0:8, :]
        own_ref[pl.ds(k, 8, stride=rows // 8), :] = home_box[k, 8:16, :]

    @pl.when(me > 0)
    def _():
        flows(me).wait_recv()

    @pl.when(me == 0)
    def _():
        arrived_ref[...] = jnp.zeros(arrived_ref.shape, F32)

    @pl.when(me < count - 1)
    def _():
        flows(me + 1).wait_send()

    for i in range(1, count):
        peer = lax.rem(me + i, count)
        outward(peer, me).wait_send()
        homeward(peer, me).wait_send()


def final_kernel(
    local_ref, gain_ref, flow_ref, lateral_ref, rough_ref, factor_ref, down_ref, inlet_ref, outer_ref, own_ref,
    arrived_ref, grad_ref, rough_grad_ref,
):
    step = pl.program_id(0)
    levels, members = flow_ref.shape[0], flow_ref.shape[1]
    steps = levels - 1
    outer_high, outer_low = split(outer_ref[...])
    outer = jnp.concatenate([outer_high, outer_low], 0)
    arrived = arrived_ref[...].reshape(levels, members, LANES)
    own = own_ref[...].reshape(steps, members, LANES)
    boundary = jnp.sum(
        jnp.sum(own * (-0.5 * arrived[1:] - 0.3 * arrived[:steps]), axis=0), axis=0, keepdims=True
    )
    boundary_high = boundary.astype(BF16).astype(F32)
    boundary = rows_of([boundary_high, boundary - boundary_high]).astype(BF16)
    inlet = inlet_ref[...]
    for j in range(GROUP):
        lanes = slice(j * LANES, (j + 1) * LANES)
        divisor = 0.8 * (rough_ref[j : j + 1, :] * factor_ref[j : j + 1, :]) + 0.5
        side = 1.0 / divisor
        scale = factor_ref[j : j + 1, :] / (divisor * divisor)
        slot = gain_ref[4:5, lanes]
        number = lax.broadcasted_iota(jnp.int32, (LANES, LANES), 0).astype(F32) + 1.0
        picked = jnp.where(number == slot, 1.0, 0.0).astype(BF16)
        taken = dot(outer, picked)
        rows = taken.shape[0] // 2
        taken = (taken[:rows] + taken[rows:]).reshape(steps, members, LANES)
        flow = flow_ref[:, :, lanes]
        inflow = dot_t(flow.reshape(levels * members, LANES), one_hot(down_ref[j : j + 1, :], 0))
        inflow = inflow.reshape(levels, members, LANES)
        total = jnp.zeros((members, LANES), F32)
        for t in range(steps):
            adjoint = local_ref[t, :, lanes]
            for d in range(steps - t):
                adjoint = adjoint + gain_ref[d : d + 1, lanes] * taken[t + d]
            grad_ref[t, :, lanes] = (side * adjoint).astype(BF16)
            held = flow[t].astype(F32) - lateral_ref[t, :, lanes].astype(F32)
            total = total + adjoint * (0.8 * held - 0.5 * inflow[t + 1] - 0.3 * inflow[t])
        placed = dot_t(boundary, one_hot(inlet, (step * GROUP + j) * LANES))
        rough_grad_ref[j : j + 1, :] = scale * (jnp.sum(total, axis=0, keepdims=True) + placed[0:1] + placed[1:2])


def sum_kernel(partial_ref, out_ref, out_box, in_box, send, recv):
    count = out_box.shape[0]
    me = lax.axis_index("mem")
    barrier = pltpu.get_barrier_semaphore()
    for i in range(1, count):
        peer = lax.rem(me + i, count)
        pl.semaphore_signal(barrier, inc=1, device_id={"mem": peer}, device_id_type=MESH)
    for k in range(count):
        out_box[k, 0:2, :] = partial_ref[2 * k : 2 * k + 2, :]
        out_box[k, 2:8, :] = jnp.zeros((6, LANES), F32)
    in_box[me] = out_box[me]
    pl.semaphore_wait(barrier, count - 1)

    def copy(peer, slot):
        return pltpu.make_async_remote_copy(
            src_ref=out_box.at[peer], dst_ref=in_box.at[slot], send_sem=send.at[peer], recv_sem=recv.at[slot],
            device_id={"mem": peer}, device_id_type=MESH,
        )

    for i in range(1, count):
        copy(lax.rem(me + i, count), me).start()
    for i in range(1, count):
        peer = lax.rem(me + i, count)
        copy(peer, peer).wait_recv()
    total = in_box[0]
    for k in range(1, count):
        total = total + in_box[k]
    out_ref[...] = total[0:2]
    for i in range(1, count):
        copy(lax.rem(me + i, count), me).wait_send()


def body(stored_reach_flows, lateral, cotangent, roughness, travel_factor, inverse_block_matrix, down_in_block, exit_slot, inlet_reach):
    steps, members, reaches = cotangent.shape
    levels = steps + 1
    blocks = reaches // LANES
    net, mem = lax.axis_size("net"), lax.axis_size("mem")
    rough = roughness.reshape(blocks, LANES)
    factor = travel_factor.reshape(blocks, LANES)
    down = down_in_block.reshape(blocks, LANES)
    exits = exit_slot.reshape(blocks, LANES)
    wide = GROUP * LANES

    def rows3(first):
        return pl.BlockSpec((first, members, wide), lambda g: (0, 0, g))

    per_block = pl.BlockSpec((GROUP, LANES), lambda g: (g, 0))

    def whole(*shape):
        return pl.BlockSpec(shape, lambda g: (0,) * len(shape))

    local, gain, inner, leaving = pl.pallas_call(
        local_kernel,
        grid=(blocks // GROUP,),
        in_specs=[
            rows3(steps), rows3(levels), per_block, per_block, per_block,
            pl.BlockSpec((GROUP, LANES, LANES), lambda g: (g, 0, 0)), whole(1, LANES),
        ],
        out_specs=[
            rows3(steps), pl.BlockSpec((8, wide), lambda g: (0, g)),
            whole(steps * members + 8, LANES), whole(levels * members, LANES),
        ],
        out_shape=[
            jax.ShapeDtypeStruct((steps, members, reaches), F32),
            jax.ShapeDtypeStruct((8, reaches), F32),
            jax.ShapeDtypeStruct((steps * members + 8, LANES), F32),
            jax.ShapeDtypeStruct((levels * members, LANES), F32),
        ],
        compiler_params=pltpu.CompilerParams(vmem_limit_bytes=40 << 20),
        name="local",
    )(cotangent, stored_reach_flows, rough, factor, exits, inverse_block_matrix, inlet_reach)

    vmem = pl.BlockSpec(memory_space=pltpu.VMEM)
    outer, own, arrived = pl.pallas_call(
        exchange_kernel,
        in_specs=[vmem] * 2,
        out_specs=[vmem] * 3,
        out_shape=[
            jax.ShapeDtypeStruct((steps * members, LANES), F32),
            jax.ShapeDtypeStruct((steps * members, LANES), F32),
            jax.ShapeDtypeStruct((levels * members, LANES), F32),
        ],
        scratch_shapes=[pltpu.VMEM((net, 16, LANES), F32)] * 4
        + [pltpu.SemaphoreType.DMA((net,))] * 4
        + [pltpu.SemaphoreType.DMA((2,))],
        compiler_params=pltpu.CompilerParams(collective_id=0, has_side_effects=True),
        name="exchange",
    )(inner, leaving)

    grad_lateral, partial = pl.pallas_call(
        final_kernel,
        grid=(blocks // GROUP,),
        in_specs=[
            rows3(steps), pl.BlockSpec((8, wide), lambda g: (0, g)), rows3(levels), rows3(steps), per_block, per_block,
            per_block, whole(1, LANES), whole(steps * members, LANES), whole(steps * members, LANES),
            whole(levels * members, LANES),
        ],
        out_specs=[rows3(steps), per_block],
        out_shape=[
            jax.ShapeDtypeStruct((steps, members, reaches), BF16),
            jax.ShapeDtypeStruct((blocks, LANES), F32),
        ],
        compiler_params=pltpu.CompilerParams(vmem_limit_bytes=40 << 20),
        name="final",
    )(local, gain, stored_reach_flows, lateral, rough, factor, down, inlet_reach, outer, own, arrived)

    grad_rough = pl.pallas_call(
        sum_kernel,
        in_specs=[vmem],
        out_specs=vmem,
        out_shape=jax.ShapeDtypeStruct((blocks // mem, LANES), F32),
        scratch_shapes=[pltpu.VMEM((mem, 8, LANES), F32)] * 2 + [pltpu.SemaphoreType.DMA((mem,))] * 2,
        compiler_params=pltpu.CompilerParams(collective_id=1, has_side_effects=True),
        name="rough_sum",
    )(partial)
    return grad_lateral, grad_rough.reshape(reaches // mem)


def solution(mesh):
    in_specs = (
        P(None, "mem", "net"),
        P(None, "mem", "net"),
        P(None, "mem", "net"),
        P("net"),
        P("net"),
        P("net", None, None),
        P("net"),
        P("net"),
        P("net", None),
    )
    out_specs = (P(None, "mem", "net"), P(("net", "mem")))
    return jax.shard_map(body, mesh=mesh, in_specs=in_specs, out_specs=out_specs, check_vma=False)
```

```python
import jax
import jax.numpy as jnp
from jax import lax
from jax.experimental import pallas as pl
from jax.experimental.pallas import tpu as pltpu
from jax.sharding import PartitionSpec as P

F32, BF16 = jnp.float32, jnp.bfloat16
LANES = 128
GROUP = 8
WIDE = GROUP * LANES
MESH = pl.DeviceIdType.MESH


def dot(a, b):
    return lax.dot_general(a, b, (((1,), (0,)), ((), ())), preferred_element_type=F32)


def dot_t(a, b):
    return lax.dot_general(a, b, (((1,), (1,)), ((), ())), preferred_element_type=F32)


def split(value):
    high = value.astype(BF16)
    return high, (value - high.astype(F32)).astype(BF16)


def stack_split(value):
    high = value.astype(BF16).astype(F32)
    return jnp.concatenate([high, value - high], 0).astype(BF16)


def halves(value):
    rows = value.shape[0] // 2
    return value[:rows] + value[rows:]


def rows_of(rows):
    place = lax.broadcasted_iota(jnp.int32, (8, LANES), 0)
    out = jnp.zeros((8, LANES), F32)
    for i, row in enumerate(rows):
        out = jnp.where(place == i, jnp.broadcast_to(row, (8, LANES)), out)
    return out


def one_hot(row, start):
    place = lax.broadcasted_iota(jnp.int32, (LANES, LANES), 0) + start
    return jnp.where(place == row, 1.0, 0.0).astype(BF16)


def pick(slot):
    number = lax.broadcasted_iota(jnp.int32, (LANES, LANES), 0).astype(F32) + 1.0
    return jnp.where(number == slot, 1.0, 0.0).astype(BF16)


def kernel(
    cot_hbm, flow_hbm, lateral_hbm, matrix_hbm, rough_hbm, factor_hbm, exits_hbm, down_hbm, inlet_hbm,
    grad, rough_out,
    cot, flow, lateral, matrix, rough, factor, exits, down, inlet,
    table, local, gain, term, inner, leaving, arrived, edge, outer,
    out_box, in_box, back_box, home_box, partial, sum_out, sum_in,
    small_sem, matrix_sem, cot_sem, flow_sem, lateral_sem,
    send, recv, back_send, back_recv, cross_sem, sum_send, sum_recv,
):
    net, mem = out_box.shape[0], sum_out.shape[0]
    steps, members, reaches = cot.shape
    levels = steps + 1
    rows = steps * members
    stride = rows // 8
    groups = reaches // WIDE
    me, you = lax.axis_index("net"), lax.axis_index("mem")

    barrier = pltpu.get_barrier_semaphore()
    for i in range(1, net):
        pl.semaphore_signal(barrier, inc=1, device_id={"net": lax.rem(me + i, net)}, device_id_type=MESH)
    for i in range(1, mem):
        pl.semaphore_signal(barrier, inc=1, device_id={"mem": lax.rem(you + i, mem)}, device_id_type=MESH)

    smalls = [
        pltpu.make_async_copy(a, b, small_sem.at[i])
        for i, (a, b) in enumerate(
            [(rough_hbm, rough), (factor_hbm, factor), (exits_hbm, exits), (inlet_hbm, inlet), (down_hbm, down)]
        )
    ]

    def lanes_of(g):
        return pl.ds(pl.multiple_of(g * WIDE, WIDE), WIDE)

    def matrix_copy(g):
        block = pl.ds(g * GROUP, GROUP)
        return pltpu.make_async_copy(matrix_hbm.at[block], matrix.at[block], matrix_sem.at[g])

    def wide_copy(source, target, sem, g):
        return pltpu.make_async_copy(source.at[:, :, lanes_of(g)], target.at[:, :, lanes_of(g)], sem.at[g])

    for copy in smalls[:4]:
        copy.start()
    for g in range(groups):
        matrix_copy(g).start()
        wide_copy(cot_hbm, cot, cot_sem, g).start()
    smalls[4].start()
    for g in range(groups):
        wide_copy(flow_hbm, flow, flow_sem, g).start()
        wide_copy(lateral_hbm, lateral, lateral_sem, g).start()

    for copy in smalls[:4]:
        copy.wait()
    travel = rough[...] * factor[...]
    divisor = 0.8 * travel + 0.5
    numer_new = 0.5 - 0.2 * travel
    numer_old = 0.5 + 0.2 * travel
    ratio = numer_old / numer_new
    side = 1.0 / divisor
    table[0] = (0.8 * travel - 0.5) / divisor + ratio
    table[1] = ratio
    table[2] = numer_new / divisor
    table[3] = numer_old / divisor
    table[4] = side
    table[5] = factor[...] / (divisor * divisor)
    inner[...] = jnp.zeros(inner.shape, F32)
    leaving[...] = jnp.zeros(leaving.shape, F32)

    def eight(ref, g):
        return ref[pl.ds(pl.multiple_of(g * GROUP, GROUP), GROUP), :]

    def solve(g, carried):
        matrix_copy(g).wait()
        wide_copy(cot_hbm, cot, cot_sem, g).wait()
        lanes = [pl.ds(pl.multiple_of(g * WIDE + j * LANES, LANES), LANES) for j in range(GROUP)]
        carry, ratio, weight_new, weight_old = (eight(table.at[k], g) for k in range(4))
        exit_rows = eight(exits, g)
        opened = jnp.where(exit_rows >= 0, 1.0, 0.0)
        numbered = jnp.where(exit_rows >= 0, exit_rows + 1, 0).astype(F32)
        weights = []
        slots = []
        for j in range(GROUP):
            block = matrix[g * GROUP + j]
            weights.append(split(block))
            pattern = jnp.where(block != 0.0, 1.0, 0.0).astype(BF16)
            slots.append(dot(jnp.broadcast_to(numbered[j : j + 1], (8, LANES)).astype(BF16), pattern)[0:1])
        adjoint = [None] * GROUP
        found = [[None] * steps for _ in range(GROUP)]
        gains = [[] for _ in range(GROUP)]
        for t in reversed(range(steps)):
            for j in range(GROUP):
                high, low = weights[j]
                start = cot[t, :, lanes[j]].astype(F32)
                if t == steps - 1:
                    x = jnp.concatenate([start, jnp.broadcast_to(opened[j : j + 1], (8, LANES))], 0).astype(BF16)
                    value = dot(x, high) + dot(x, low)
                else:
                    x = jnp.concatenate([start, jnp.zeros((8, LANES), F32)], 0) + adjoint[j] * carry[j : j + 1]
                    x_high, x_low = split(x)
                    value = dot(x_high, high) + dot(x_low, high) + dot(x_high, low) - adjoint[j] * ratio[j : j + 1]
                adjoint[j] = value
                found[j][t] = value[:members]
                local[t, :, lanes[j]] = value[:members]
                gains[j].append(value[members : members + 1])
        total = jnp.zeros(inner.shape, F32)
        for j in range(GROUP):
            facts = rows_of(gains[j] + [slots[j], weight_new[j : j + 1], weight_old[j : j + 1]])
            gain[:, lanes[j]] = facts
            both = stack_split(jnp.concatenate(found[j] + [facts], 0))
            total = total + dot(both, one_hot(inlet[...], (g * GROUP + j) * LANES))
        inner[...] += total
        return carried

    lax.fori_loop(0, groups, solve, 0)

    inside = halves(inner[...])
    facts = inside[rows:]
    inside = inside[:rows]
    weight_new, weight_old = facts[5:6], facts[6:7]
    edge[...] = weight_new * inside + weight_old * jnp.concatenate(
        [inside[members:], jnp.zeros((members, LANES), F32)], 0
    )
    passed = [weight_new * facts[0:1]] + [weight_new * facts[d : d + 1] + weight_old * facts[d - 1 : d] for d in range(1, steps)]
    message = rows_of(passed + [facts[4:5]])
    for k in range(net):
        out_box[k, 0:8, :] = edge[pl.ds(k, 8, stride=stride), :]
        out_box[k, 8:16, :] = message
    in_box[me] = out_box[me]

    def outward(peer, slot):
        return pltpu.make_async_remote_copy(
            src_ref=out_box.at[peer], dst_ref=in_box.at[slot], send_sem=send.at[peer], recv_sem=recv.at[slot],
            device_id={"net": peer}, device_id_type=MESH,
        )

    def homeward(peer, slot):
        return pltpu.make_async_remote_copy(
            src_ref=back_box.at[peer], dst_ref=home_box.at[slot], send_sem=back_send.at[peer],
            recv_sem=back_recv.at[slot], device_id={"net": peer}, device_id_type=MESH,
        )

    def across(peer):
        return pltpu.make_async_remote_copy(
            src_ref=leaving, dst_ref=arrived, send_sem=cross_sem.at[0], recv_sem=cross_sem.at[1],
            device_id={"net": peer}, device_id_type=MESH,
        )

    def sums(peer, slot):
        return pltpu.make_async_remote_copy(
            src_ref=sum_out.at[peer], dst_ref=sum_in.at[slot], send_sem=sum_send.at[peer], recv_sem=sum_recv.at[slot],
            device_id={"mem": peer}, device_id_type=MESH,
        )

    if net + mem > 2:
        pl.semaphore_wait(barrier, net + mem - 2)

    @pl.when(me > 0)
    def _():
        for i in range(1, net):
            outward(lax.rem(me + i, net), me).start()

    smalls[4].wait()

    def inflows(g, carried):
        wide_copy(flow_hbm, flow, flow_sem, g).wait()
        wide_copy(lateral_hbm, lateral, lateral_sem, g).wait()
        down_rows, exit_rows = eight(down, g), eight(exits, g)
        total = jnp.zeros(leaving.shape, F32)
        for j in range(GROUP):
            lanes = pl.ds(pl.multiple_of(g * WIDE + j * LANES, LANES), LANES)
            here = flow[:, :, lanes]
            flat = here.reshape(levels * members, LANES)
            inflow = dot_t(flat, one_hot(down_rows[j : j + 1], 0)).reshape(levels, members, LANES)
            total = total + dot_t(flat, one_hot(exit_rows[j : j + 1], 0))
            held = here[:steps].astype(F32) - lateral[:, :, lanes].astype(F32)
            term[:, :, lanes] = 0.8 * held - 0.5 * inflow[1:] - 0.3 * inflow[:steps]
        leaving[...] += total
        return carried

    lax.fori_loop(0, groups, inflows, 0)

    @pl.when(me < net - 1)
    def _():
        across(me + 1).start()

    place = lax.broadcasted_iota(jnp.int32, (8, LANES), 0)
    state = None
    for p in reversed(range(1, net)):

        @pl.when(me != p)
        def _():
            outward(p, p).wait_recv()

        own = in_box[p, 0:8, :]
        if state is not None:
            both = halves(dot(stack_split(state), pick(in_box[p, 12:13, :])))
            own = own + both * in_box[p, 8:9, :]
            for d in range(1, steps):
                later = jnp.where(place < 8 - 2 * d, pltpu.roll(both, 8 - 2 * d, 0), 0.0)
                own = own + later * in_box[p, 8 + d : 9 + d, :]
        state = own
        back_box[p - 1] = state

        @pl.when(me != p - 1)
        def _():
            homeward(p - 1, me).start()

        @pl.when(me == p - 1)
        def _():
            home_box[p - 1] = back_box[p - 1]

    @pl.when(me == net - 1)
    def _():
        outer[...] = jnp.zeros(outer.shape, F32)

    @pl.when(me < net - 1)
    def _():
        for k in range(net):

            @pl.when(me != k)
            def _():
                homeward(k, k).wait_recv()

            outer[pl.ds(k, 8, stride=stride), :] = home_box[k]

    both = stack_split(outer[...])

    def taken_at(slot):
        return halves(dot(both, pick(slot))).reshape(steps, members, LANES)

    def finish(g, carried):
        side, scale = eight(table.at[4], g), eight(table.at[5], g)
        out = []
        for j in range(GROUP):
            lanes = pl.ds(pl.multiple_of(g * WIDE + j * LANES, LANES), LANES)
            facts = gain[:, lanes]
            taken = taken_at(facts[4:5])
            total = jnp.zeros((members, LANES), F32)
            for t in range(steps):
                adjoint = local[t, :, lanes]
                for d in range(steps - t):
                    adjoint = adjoint + facts[d : d + 1] * taken[t + d]
                grad[t, :, lanes] = (side[j : j + 1] * adjoint).astype(BF16)
                total = total + adjoint * term[t, :, lanes]
            out.append(jnp.sum(total, axis=0, keepdims=True))
        partial[pl.ds(pl.multiple_of(g * GROUP, GROUP), GROUP), :] = rows_of(out)
        return carried

    lax.fori_loop(0, groups, finish, 0)

    @pl.when(me > 0)
    def _():
        across(me).wait_recv()

    @pl.when(me == 0)
    def _():
        arrived[...] = jnp.zeros(arrived.shape, F32)

    came = arrived[...].reshape(levels, members, LANES)
    came = -0.5 * came[1:] - 0.3 * came[:steps]
    taken = taken_at(facts[4:5])
    total = jnp.zeros((members, LANES), F32)
    for t in range(steps):
        adjoint = inside[t * members : (t + 1) * members]
        for d in range(steps - t):
            adjoint = adjoint + facts[d : d + 1] * taken[t + d]
        total = total + adjoint * came[t]
    total = jnp.sum(total, axis=0, keepdims=True)
    high = total.astype(BF16).astype(F32)
    total = rows_of([high, total - high]).astype(BF16)
    within = lax.broadcasted_iota(jnp.int32, (LANES, LANES), 0)
    lane = lax.broadcasted_iota(jnp.int32, (8, LANES), 1)
    for g in range(groups):
        out = []
        for h in range(GROUP // 4):
            first = (g * GROUP + h * 4) * LANES
            near = jnp.where(within // 32 * LANES + within % 32 + first == inlet[...], 1.0, 0.0).astype(BF16)
            placed = dot_t(total, near)
            placed = placed + pltpu.roll(placed, 7, 0)
            for i in range(4):
                shifted = placed if i == 0 else pltpu.roll(placed, LANES - 32 * i, 1)
                out.append(jnp.where(lane < 32, shifted, 0.0)[0:1])
        here = pl.ds(g * GROUP, GROUP)
        partial[here, :] = (partial[here, :] + rows_of(out)) * table[5, here, :]

    for k in range(mem):
        sum_out[k] = jnp.zeros((8, LANES), F32)
        sum_out[k, 0:2, :] = partial[2 * k : 2 * k + 2, :]
    sum_in[you] = sum_out[you]
    for i in range(1, mem):
        sums(lax.rem(you + i, mem), you).start()
    for i in range(1, mem):
        peer = lax.rem(you + i, mem)
        sums(peer, peer).wait_recv()
    total = sum_in[0]
    for k in range(1, mem):
        total = total + sum_in[k]
    rough_out[...] = total[0:2]

    for i in range(1, mem):
        sums(lax.rem(you + i, mem), you).wait_send()

    @pl.when(me > 0)
    def _():
        for i in range(1, net):
            outward(lax.rem(me + i, net), me).wait_send()

    @pl.when(me < net - 1)
    def _():
        across(me + 1).wait_send()

    for p in range(net - 1):

        @pl.when(me != p)
        def _():
            homeward(p, me).wait_send()


def body(stored_reach_flows, lateral, cotangent, roughness, travel_factor, inverse_block_matrix, down_in_block, exit_slot, inlet_reach):
    steps, members, reaches = cotangent.shape
    levels = steps + 1
    blocks = reaches // LANES
    groups = reaches // WIDE
    net, mem = lax.axis_size("net"), lax.axis_size("mem")

    def blocked(value):
        return value.reshape(blocks, LANES)

    anywhere = pl.BlockSpec(memory_space=pltpu.HBM)
    vmem = pl.BlockSpec(memory_space=pltpu.VMEM)
    dma = pltpu.SemaphoreType.DMA
    shaped = pltpu.VMEM
    per_block = [shaped((blocks, LANES), F32)] * 2 + [shaped((blocks, LANES), jnp.int32)]
    grad_lateral, grad_rough = pl.pallas_call(
        kernel,
        in_specs=[anywhere] * 9,
        out_specs=[vmem, vmem],
        out_shape=[
            jax.ShapeDtypeStruct((steps, members, reaches), BF16),
            jax.ShapeDtypeStruct((2, LANES), F32),
        ],
        scratch_shapes=[
            shaped((steps, members, reaches), BF16),
            shaped((levels, members, reaches), BF16),
            shaped((steps, members, reaches), BF16),
            shaped((blocks, LANES, LANES), F32),
            *per_block,
            shaped((blocks, LANES), jnp.int32),
            shaped((1, LANES), jnp.int32),
            shaped((6, blocks, LANES), F32),
            shaped((steps, members, reaches), F32),
            shaped((8, reaches), F32),
            shaped((steps, members, reaches), F32),
            shaped((2 * (steps * members + 8), LANES), F32),
            shaped((levels * members, LANES), F32),
            shaped((levels * members, LANES), F32),
            shaped((steps * members, LANES), F32),
            shaped((steps * members, LANES), F32),
            shaped((net, 16, LANES), F32),
            shaped((net, 16, LANES), F32),
            shaped((net, 8, LANES), F32),
            shaped((net, 8, LANES), F32),
            shaped((blocks, LANES), F32),
            shaped((mem, 8, LANES), F32),
            shaped((mem, 8, LANES), F32),
            dma((5,)), dma((groups,)), dma((groups,)), dma((groups,)), dma((groups,)),
            dma((net,)), dma((net,)), dma((net,)), dma((net,)), dma((2,)), dma((mem,)), dma((mem,)),
        ],
        compiler_params=pltpu.CompilerParams(collective_id=0, has_side_effects=True, vmem_limit_bytes=56 << 20),
        name="adjoint",
    )(
        cotangent, stored_reach_flows, lateral, inverse_block_matrix, blocked(roughness), blocked(travel_factor),
        blocked(exit_slot), blocked(down_in_block), inlet_reach,
    )
    return grad_lateral, grad_rough.reshape(2 * LANES)


def solution(mesh):
    in_specs = (
        P(None, "mem", "net"),
        P(None, "mem", "net"),
        P(None, "mem", "net"),
        P("net"),
        P("net"),
        P("net", None, None),
        P("net"),
        P("net"),
        P("net", None),
    )
    out_specs = (P(None, "mem", "net"), P(("net", "mem")))
    return jax.shard_map(body, mesh=mesh, in_specs=in_specs, out_specs=out_specs, check_vma=False)
```

```python
import jax
import jax.numpy as jnp
from jax import lax
from jax.experimental import pallas as pl
from jax.experimental.pallas import tpu as pltpu
from jax.sharding import PartitionSpec as P

F32, BF16 = jnp.float32, jnp.bfloat16
LANES = 128
GROUP = 8
WIDE = GROUP * LANES
MESH = pl.DeviceIdType.MESH


def dot(a, b):
    return lax.dot_general(a, b, (((1,), (0,)), ((), ())), preferred_element_type=F32)


def dot_t(a, b):
    return lax.dot_general(a, b, (((1,), (1,)), ((), ())), preferred_element_type=F32)


def split(value):
    high = value.astype(BF16)
    return high, (value - high.astype(F32)).astype(BF16)


def stack_split(value):
    high = value.astype(BF16).astype(F32)
    return jnp.concatenate([high, value - high], 0).astype(BF16)


def halves(value):
    rows = value.shape[0] // 2
    return value[:rows] + value[rows:]


def rows_of(rows):
    place = lax.broadcasted_iota(jnp.int32, (8, LANES), 0)
    out = jnp.zeros((8, LANES), F32)
    for i, row in enumerate(rows):
        out = jnp.where(place == i, jnp.broadcast_to(row, (8, LANES)), out)
    return out


def one_hot(row, start):
    place = lax.broadcasted_iota(jnp.int32, (LANES, LANES), 0) + start
    return jnp.where(place == row, 1.0, 0.0).astype(BF16)


def pick(slot):
    number = lax.broadcasted_iota(jnp.int32, (LANES, LANES), 0).astype(F32) + 1.0
    return jnp.where(number == slot, 1.0, 0.0).astype(BF16)


def kernel(
    cot_hbm, flow_hbm, lateral_hbm, matrix_hbm, rough_hbm, factor_hbm, exits_hbm, down_hbm, inlet_hbm,
    grad, rough_out,
    cot, flow, lateral, matrix, rough, factor, exits, down, inlet,
    table, local, gain, term, taken, inner, leaving, arrived, edge, outer,
    out_box, in_box, back_box, home_box, partial, sum_out, sum_in,
    small_sem, matrix_sem, cot_sem, flow_sem, lateral_sem,
    send, recv, back_send, back_recv, cross_sem, sum_send, sum_recv,
):
    net, mem = out_box.shape[0], sum_out.shape[0]
    steps, members, reaches = cot.shape
    levels = steps + 1
    rows = steps * members
    stride = rows // 8
    groups = reaches // WIDE
    me, you = lax.axis_index("net"), lax.axis_index("mem")

    smalls = [
        pltpu.make_async_copy(a, b, small_sem.at[i])
        for i, (a, b) in enumerate(
            [(rough_hbm, rough), (factor_hbm, factor), (exits_hbm, exits), (inlet_hbm, inlet), (down_hbm, down)]
        )
    ]

    def lanes_of(g):
        return pl.ds(pl.multiple_of(g * WIDE, WIDE), WIDE)

    def matrix_copy(g):
        block = pl.ds(g * GROUP, GROUP)
        return pltpu.make_async_copy(matrix_hbm.at[block], matrix.at[block], matrix_sem.at[g])

    def wide_copy(source, target, sem, g):
        return pltpu.make_async_copy(source.at[:, :, lanes_of(g)], target.at[:, :, lanes_of(g)], sem.at[g])

    for copy in smalls[:4]:
        copy.start()
    for g in range(groups):
        matrix_copy(g).start()
        wide_copy(cot_hbm, cot, cot_sem, g).start()
    smalls[4].start()
    for g in range(groups):
        wide_copy(flow_hbm, flow, flow_sem, g).start()
        wide_copy(lateral_hbm, lateral, lateral_sem, g).start()

    barrier = pltpu.get_barrier_semaphore()
    for i in range(1, net):
        pl.semaphore_signal(barrier, inc=1, device_id={"net": lax.rem(me + i, net)}, device_id_type=MESH)
    for i in range(1, mem):
        pl.semaphore_signal(barrier, inc=1, device_id={"mem": lax.rem(you + i, mem)}, device_id_type=MESH)

    for copy in smalls[:4]:
        copy.wait()
    travel = rough[...] * factor[...]
    divisor = 0.8 * travel + 0.5
    numer_new = 0.5 - 0.2 * travel
    numer_old = 0.5 + 0.2 * travel
    ratio = numer_old / numer_new
    side = 1.0 / divisor
    table[0] = (0.8 * travel - 0.5) / divisor + ratio
    table[1] = ratio
    table[2] = numer_new / divisor
    table[3] = numer_old / divisor
    table[4] = side
    table[5] = factor[...] / (divisor * divisor)
    inner[...] = jnp.zeros(inner.shape, F32)
    leaving[...] = jnp.zeros(leaving.shape, F32)

    def eight(ref, g):
        return ref[pl.ds(pl.multiple_of(g * GROUP, GROUP), GROUP), :]

    def solve(g, carried):
        matrix_copy(g).wait()
        wide_copy(cot_hbm, cot, cot_sem, g).wait()
        lanes = [pl.ds(pl.multiple_of(g * WIDE + j * LANES, LANES), LANES) for j in range(GROUP)]
        carry, ratio, weight_new, weight_old = (eight(table.at[k], g) for k in range(4))
        exit_rows = eight(exits, g)
        opened = jnp.where(exit_rows >= 0, 1.0, 0.0)
        numbered = jnp.where(exit_rows >= 0, exit_rows + 1, 0).astype(F32)
        weights, twice, whole = [], [], []
        slots = []
        for j in range(GROUP):
            block = matrix[g * GROUP + j]
            weights.append(split(block))
            twice.append(jnp.concatenate([weights[-1][0]] * 2, 0))
            whole.append(jnp.concatenate(weights[-1], 0))
            pattern = jnp.where(block != 0.0, 1.0, 0.0).astype(BF16)
            slots.append(dot(jnp.broadcast_to(numbered[j : j + 1], (8, LANES)).astype(BF16), pattern)[0:1])
        adjoint = [None] * GROUP
        found = [[None] * steps for _ in range(GROUP)]
        gains = [[] for _ in range(GROUP)]
        for t in reversed(range(steps)):
            for j in range(GROUP):
                high, low = weights[j]
                start = cot[t, :, lanes[j]].astype(F32)
                if t == steps - 1:
                    x = jnp.concatenate([start, jnp.broadcast_to(opened[j : j + 1], (8, LANES))], 0).astype(BF16)
                    value = dot(jnp.concatenate([x, x], 1), whole[j])
                else:
                    x = jnp.concatenate([start, jnp.zeros((8, LANES), F32)], 0) + adjoint[j] * carry[j : j + 1]
                    x_high, x_low = split(x)
                    value = dot(jnp.concatenate([x_high, x_low], 1), twice[j]) + dot(x_high, low) - adjoint[j] * ratio[j : j + 1]
                adjoint[j] = value
                found[j][t] = value[:members]
                local[t, :, lanes[j]] = value[:members]
                gains[j].append(value[members : members + 1])
        pieces, marks = [], []
        for j in range(GROUP):
            facts = rows_of(gains[j] + [slots[j], weight_new[j : j + 1], weight_old[j : j + 1]])
            gain[:, lanes[j]] = facts
            both = split(jnp.concatenate(found[j] + [facts], 0))
            mark = one_hot(inlet[...], (g * GROUP + j) * LANES)
            pieces += both
            marks += [mark, mark]
        inner[...] += dot(jnp.concatenate(pieces, 1), jnp.concatenate(marks, 0))
        return carried

    lax.fori_loop(0, groups, solve, 0)

    inside = inner[...]
    facts = inside[rows:]
    inside = inside[:rows]
    weight_new, weight_old = facts[5:6], facts[6:7]
    edge[...] = weight_new * inside + weight_old * jnp.concatenate(
        [inside[members:], jnp.zeros((members, LANES), F32)], 0
    )
    passed = [weight_new * facts[0:1]] + [weight_new * facts[d : d + 1] + weight_old * facts[d - 1 : d] for d in range(1, steps)]
    message = rows_of(passed + [facts[4:5]])
    for k in range(net):
        out_box[k, 0:8, :] = edge[pl.ds(k, 8, stride=stride), :]
        out_box[k, 8:16, :] = message
    in_box[me] = out_box[me]

    far = sorted(range(net), key=lambda i: -(2 * (i % 2) + min(i // 2, net // 2 - i // 2)))
    high, low = me // 2, lax.rem(me, 2)

    def peer_at(i):
        return 2 * lax.rem(high + i // 2, net // 2) + lax.rem(low + i % 2, 2)

    def outward(peer, slot):
        return pltpu.make_async_remote_copy(
            src_ref=out_box.at[peer], dst_ref=in_box.at[slot], send_sem=send.at[peer], recv_sem=recv.at[slot],
            device_id={"net": peer}, device_id_type=MESH,
        )

    def homeward(peer, slot):
        return pltpu.make_async_remote_copy(
            src_ref=back_box.at[peer], dst_ref=home_box.at[slot], send_sem=back_send.at[peer],
            recv_sem=back_recv.at[slot], device_id={"net": peer}, device_id_type=MESH,
        )

    def across(peer):
        return pltpu.make_async_remote_copy(
            src_ref=leaving, dst_ref=arrived, send_sem=cross_sem.at[0], recv_sem=cross_sem.at[1],
            device_id={"net": peer}, device_id_type=MESH,
        )

    def sums(peer, slot):
        return pltpu.make_async_remote_copy(
            src_ref=sum_out.at[peer], dst_ref=sum_in.at[slot], send_sem=sum_send.at[peer], recv_sem=sum_recv.at[slot],
            device_id={"mem": peer}, device_id_type=MESH,
        )

    if net + mem > 2:
        pl.semaphore_wait(barrier, net + mem - 2)

    @pl.when(me > 0)
    def _():
        for i in far[:-1]:
            outward(peer_at(i), me).start()

    smalls[4].wait()

    def inflows(g, carried):
        wide_copy(flow_hbm, flow, flow_sem, g).wait()
        wide_copy(lateral_hbm, lateral, lateral_sem, g).wait()
        down_rows, exit_rows = eight(down, g), eight(exits, g)
        marks, out = [], []
        for j in range(GROUP):
            lanes = pl.ds(pl.multiple_of(g * WIDE + j * LANES, LANES), LANES)
            here = flow[:, :, lanes]
            flat = here.reshape(levels * members, LANES)
            inflow = dot_t(flat, one_hot(down_rows[j : j + 1], 0)).reshape(levels, members, LANES)
            marks.append(one_hot(exit_rows[j : j + 1], 0))
            facts = gain[:, lanes]
            held = here[:steps].astype(F32) - lateral[:, :, lanes].astype(F32)
            terms = 0.8 * held - 0.5 * inflow[1:] - 0.3 * inflow[:steps]
            out.append(jnp.sum(jnp.sum(terms * local[:, :, lanes], axis=0), axis=0, keepdims=True))
            for t in range(steps):
                weighted = terms[t] * facts[0:1]
                for d in range(1, t + 1):
                    weighted = weighted + terms[t - d] * facts[d : d + 1]
                term[t, :, lanes] = weighted
        partial[pl.ds(pl.multiple_of(g * GROUP, GROUP), GROUP), :] = rows_of(out)
        flat = flow[:, :, lanes_of(g)].reshape(levels * members, WIDE)
        leaving[...] += dot_t(flat, jnp.concatenate(marks, 1))
        return carried

    lax.fori_loop(0, groups, inflows, 0)

    @pl.when(me < net - 1)
    def _():
        across(me + 1).start()

    for p in range(1, net):

        @pl.when(me != p)
        def _():
            outward(p, p).wait_recv()

    place = lax.broadcasted_iota(jnp.int32, (8, LANES), 0)
    state = in_box[net - 1, 0:8, :]
    back_box[net - 2] = state
    for p in reversed(range(1, net - 1)):
        slot = jnp.maximum(in_box[p, 12:13, :].astype(jnp.int32) - 1, 0)
        both = jnp.take_along_axis(state, jnp.broadcast_to(slot, (8, LANES)), axis=1, mode="promise_in_bounds")
        state = in_box[p, 0:8, :] + both * in_box[p, 8:9, :]
        for d in range(1, steps):
            passed = jnp.where(place < 8 - 2 * d, in_box[p, 8 + d : 9 + d, :], 0.0)
            state = state + pltpu.roll(both, 8 - 2 * d, 0) * passed
        back_box[p - 1] = state

    home_box[me] = back_box[me]
    for i in far[:-1]:
        peer = peer_at(i)

        @pl.when(peer < net - 1)
        def _():
            homeward(peer, me).start()

    @pl.when(me > 0)
    def _():
        across(me).wait_recv()

    @pl.when(me == 0)
    def _():
        arrived[...] = jnp.zeros(arrived.shape, F32)

    came = arrived[...].reshape(levels, members, LANES)
    came = -0.5 * came[1:] - 0.3 * came[:steps]
    boundary = jnp.sum(came * inside.reshape(steps, members, LANES), axis=0)
    crossing = []
    for t in range(steps):
        weighted = came[t] * facts[0:1]
        for d in range(1, t + 1):
            weighted = weighted + came[t - d] * facts[d : d + 1]
        crossing.append(weighted)
    crossing = jnp.concatenate(crossing, 0)

    @pl.when(me == net - 1)
    def _():
        outer[...] = jnp.zeros(outer.shape, F32)

    @pl.when(me < net - 1)
    def _():
        for k in range(net):

            @pl.when(me != k)
            def _():
                homeward(k, k).wait_recv()

            outer[pl.ds(k, 8, stride=stride), :] = home_box[k]

    both = jnp.concatenate(split(outer[...]), 1)

    def taken_at(slots):
        picked = jnp.concatenate([pick(slot) for slot in slots], 1)
        return dot(both, jnp.concatenate([picked, picked], 0))

    def weigh(g, carried):
        out = []
        for j in range(0, GROUP, 2):
            lanes = pl.ds(pl.multiple_of(g * WIDE + j * LANES, 2 * LANES), 2 * LANES)
            slots = gain[4:5, lanes]
            value = taken_at([slots[:, :LANES], slots[:, LANES:]]).reshape(steps, members, 2 * LANES)
            taken[:, :, lanes] = value
            value = jnp.sum(jnp.sum(value * term[:, :, lanes], axis=0), axis=0, keepdims=True)
            out += [value[:, :LANES], value[:, LANES:]]
        here = pl.ds(pl.multiple_of(g * GROUP, GROUP), GROUP)
        partial[here, :] += rows_of(out)
        return carried

    lax.fori_loop(0, groups, weigh, 0)

    total = jnp.sum(taken_at([facts[4:5]]) * crossing, axis=0, keepdims=True) + jnp.sum(boundary, axis=0, keepdims=True)
    size = partial.shape[0] // mem
    for k in range(mem):
        sum_out[k, 0:size, :] = partial[k * size : (k + 1) * size, :]
        sum_out[k, size : size + 1, :] = total
        sum_out[k, size + 1 :, :] = jnp.zeros((sum_out.shape[1] - size - 1, LANES), F32)
    sum_in[you] = sum_out[you]
    for i in range(1, mem):
        sums(lax.rem(you + i, mem), you).start()

    def finish(g, carried):
        side = eight(table.at[4], g)
        for j in range(GROUP):
            lanes = pl.ds(pl.multiple_of(g * WIDE + j * LANES, LANES), LANES)
            facts = gain[:, lanes]
            value = taken[:, :, lanes]
            for t in range(steps):
                adjoint = local[t, :, lanes]
                for d in range(steps - t):
                    adjoint = adjoint + facts[d : d + 1] * value[t + d]
                grad[t, :, lanes] = (side[j : j + 1] * adjoint).astype(BF16)
        return carried

    lax.fori_loop(0, groups, finish, 0)

    for i in range(1, mem):
        peer = lax.rem(you + i, mem)
        sums(peer, peer).wait_recv()
    total = sum_in[0]
    for k in range(1, mem):
        total = total + sum_in[k]
    edge_row = total[size : size + 1]
    edge_high = edge_row.astype(BF16).astype(F32)
    edge_row = rows_of([edge_high, edge_row - edge_high]).astype(BF16)
    for i in range(size):
        block = you * size + i
        placed = dot_t(edge_row, one_hot(inlet[...], block * LANES))
        rough_out[i : i + 1, :] = (total[i : i + 1] + placed[0:1] + placed[1:2]) * table[5, pl.ds(block, 1), :]

    for i in range(1, mem):
        sums(lax.rem(you + i, mem), you).wait_send()

    @pl.when(me > 0)
    def _():
        for i in far[:-1]:
            outward(peer_at(i), me).wait_send()

    @pl.when(me < net - 1)
    def _():
        across(me + 1).wait_send()

    for i in far[:-1]:
        peer = peer_at(i)

        @pl.when(peer < net - 1)
        def _():
            homeward(peer, me).wait_send()


def store_kernel(grad, rough, grad_out, rough_out, sem):
    copies = [
        pltpu.make_async_copy(grad, grad_out, sem.at[0]),
        pltpu.make_async_copy(rough, rough_out, sem.at[1]),
    ]
    for copy in copies:
        copy.start()
    for copy in copies:
        copy.wait()


def body(stored_reach_flows, lateral, cotangent, roughness, travel_factor, inverse_block_matrix, down_in_block, exit_slot, inlet_reach):
    steps, members, reaches = cotangent.shape
    levels = steps + 1
    blocks = reaches // LANES
    groups = reaches // WIDE
    net, mem = lax.axis_size("net"), lax.axis_size("mem")

    def blocked(value):
        return value.reshape(blocks, LANES)

    anywhere = pl.BlockSpec(memory_space=pltpu.HBM)
    vmem = pl.BlockSpec(memory_space=pltpu.VMEM)
    dma = pltpu.SemaphoreType.DMA
    shaped = pltpu.VMEM
    per_block = [shaped((blocks, LANES), F32)] * 2 + [shaped((blocks, LANES), jnp.int32)]
    grad_lateral, grad_rough = pl.pallas_call(
        kernel,
        in_specs=[anywhere] * 9,
        out_specs=[vmem, vmem],
        out_shape=[
            pltpu.VMEM((steps, members, reaches), BF16),
            pltpu.VMEM((blocks // mem, LANES), F32),
        ],
        scratch_shapes=[
            shaped((steps, members, reaches), BF16),
            shaped((levels, members, reaches), BF16),
            shaped((steps, members, reaches), BF16),
            shaped((blocks, LANES, LANES), F32),
            *per_block,
            shaped((blocks, LANES), jnp.int32),
            shaped((1, LANES), jnp.int32),
            shaped((6, blocks, LANES), F32),
            shaped((steps, members, reaches), F32),
            shaped((8, reaches), F32),
            shaped((steps, members, reaches), F32),
            shaped((steps, members, reaches), F32),
            shaped((steps * members + 8, LANES), F32),
            shaped((levels * members, LANES), F32),
            shaped((levels * members, LANES), F32),
            shaped((steps * members, LANES), F32),
            shaped((steps * members, LANES), F32),
            shaped((net, 16, LANES), F32),
            shaped((net, 16, LANES), F32),
            shaped((net, 8, LANES), F32),
            shaped((net, 8, LANES), F32),
            shaped((blocks, LANES), F32),
            shaped((mem, 4, LANES), F32),
            shaped((mem, 4, LANES), F32),
            dma((5,)), dma((groups,)), dma((groups,)), dma((groups,)), dma((groups,)),
            dma((net,)), dma((net,)), dma((net,)), dma((net,)), dma((2,)), dma((mem,)), dma((mem,)),
        ],
        compiler_params=pltpu.CompilerParams(collective_id=0, has_side_effects=True, vmem_limit_bytes=56 << 20),
        name="adjoint",
    )(
        cotangent, stored_reach_flows, lateral, inverse_block_matrix, blocked(roughness), blocked(travel_factor),
        blocked(exit_slot), blocked(down_in_block), inlet_reach,
    )
    grad_lateral, grad_rough = pl.pallas_call(
        store_kernel,
        in_specs=[vmem, vmem],
        out_specs=[anywhere, anywhere],
        out_shape=[
            jax.ShapeDtypeStruct(grad_lateral.shape, BF16),
            jax.ShapeDtypeStruct(grad_rough.shape, F32),
        ],
        scratch_shapes=[dma((2,))],
        compiler_params=pltpu.CompilerParams(vmem_limit_bytes=4 << 20),
        name="store",
    )(grad_lateral, grad_rough)
    return grad_lateral, grad_rough.reshape(reaches // mem)


def solution(mesh):
    in_specs = (
        P(None, "mem", "net"),
        P(None, "mem", "net"),
        P(None, "mem", "net"),
        P("net"),
        P("net"),
        P("net", None, None),
        P("net"),
        P("net"),
        P("net", None),
    )
    out_specs = (P(None, "mem", "net"), P(("net", "mem")))
    return jax.shard_map(body, mesh=mesh, in_specs=in_specs, out_specs=out_specs, check_vma=False)
```

```python
import jax
import jax.numpy as jnp
from jax import lax
from jax.experimental import pallas as pl
from jax.experimental.pallas import tpu as pltpu
from jax.sharding import PartitionSpec as P

F32, BF16 = jnp.float32, jnp.bfloat16
LANES = 128
GROUP = 16
WIDE = GROUP * LANES
MESH = pl.DeviceIdType.MESH


def dot(a, b):
    return lax.dot_general(a, b, (((1,), (0,)), ((), ())), preferred_element_type=F32)


def dot_t(a, b):
    return lax.dot_general(a, b, (((1,), (1,)), ((), ())), preferred_element_type=F32)


def split(value):
    high = value.astype(BF16)
    return high, (value - high.astype(F32)).astype(BF16)


def stack_split(value):
    high = value.astype(BF16).astype(F32)
    return jnp.concatenate([high, value - high], 0).astype(BF16)


def halves(value):
    rows = value.shape[0] // 2
    return value[:rows] + value[rows:]


def rows_of(rows):
    if len(rows) > 8:
        return jnp.concatenate([rows_of(rows[:8]), rows_of(rows[8:])], 0)
    place = lax.broadcasted_iota(jnp.int32, (8, LANES), 0)
    out = jnp.zeros((8, LANES), F32)
    for i, row in enumerate(rows):
        out = jnp.where(place == i, jnp.broadcast_to(row, (8, LANES)), out)
    return out


def one_hot(row, start):
    place = lax.broadcasted_iota(jnp.int32, (LANES, LANES), 0) + start
    return jnp.where(place == row, 1.0, 0.0).astype(BF16)


def gather(value, row):
    return jnp.take_along_axis(value, jnp.broadcast_to(row, value.shape), axis=1, mode="promise_in_bounds")


def kernel(
    cot_hbm, flow_hbm, lateral_hbm, matrix_hbm, rough_hbm, factor_hbm, exits_hbm, down_hbm, inlet_hbm,
    grad, rough_out,
    cot, flow, lateral, matrix, rough, factor, exits, down, inlet,
    table, local, gain, term, taken, inner, leaving, passing, arrived, edge, outer,
    out_box, in_box, back_box, home_box, partial, sum_out, sum_in,
    small_sem, matrix_sem, cot_sem, flow_sem, lateral_sem,
    send, recv, back_send, back_recv, cross_sem, sum_send, sum_recv,
):
    net, mem = out_box.shape[0], sum_out.shape[0]
    steps, members, reaches = cot.shape
    levels = steps + 1
    rows = steps * members
    stride = rows // 8
    groups = reaches // WIDE
    me, you = lax.axis_index("net"), lax.axis_index("mem")

    near = sorted(range(1, mem), key=lambda i: -(i // 8 + min(i % 8 // 2, 4 - i % 8 // 2)))

    def mate_at(i):
        y = lax.rem(lax.rem(you // 2, 4) + i % 8 // 2, 4)
        return lax.rem(you // 8 + i // 8, 2) * 8 + y * 2 + lax.rem(lax.rem(you, 2) + i % 2, 2)

    far = sorted(range(net), key=lambda i: -(2 * (i % 2) + min(i // 2, net // 2 - i // 2)))
    high, low = me // 2, lax.rem(me, 2)

    def peer_at(i):
        return 2 * lax.rem(high + i // 2, net // 2) + lax.rem(low + i % 2, 2)

    barrier = pltpu.get_barrier_semaphore()
    for i in far[:-1]:
        pl.semaphore_signal(barrier, inc=1, device_id={"net": peer_at(i)}, device_id_type=MESH)

    smalls = [
        pltpu.make_async_copy(a, b, small_sem.at[i])
        for i, (a, b) in enumerate(
            [(rough_hbm, rough), (factor_hbm, factor), (exits_hbm, exits), (inlet_hbm, inlet), (down_hbm, down)]
        )
    ]

    def lanes_of(g):
        return pl.ds(pl.multiple_of(g * WIDE, WIDE), WIDE)

    def matrix_copy(g):
        block = pl.ds(g * GROUP, GROUP)
        return pltpu.make_async_copy(matrix_hbm.at[block], matrix.at[block], matrix_sem.at[g])

    def wide_copy(source, target, sem, g):
        return pltpu.make_async_copy(source.at[:, :, lanes_of(g)], target.at[:, :, lanes_of(g)], sem.at[g])

    for copy in smalls[:4]:
        copy.start()
    for g in range(groups):
        matrix_copy(g).start()
        wide_copy(cot_hbm, cot, cot_sem, g).start()
    for i in near:
        pl.semaphore_signal(barrier, inc=1, device_id={"mem": mate_at(i)}, device_id_type=MESH)
    smalls[4].start()
    for g in range(groups):
        wide_copy(flow_hbm, flow, flow_sem, g).start()
        wide_copy(lateral_hbm, lateral, lateral_sem, g).start()

    for copy in smalls[:4]:
        copy.wait()
    travel = rough[...] * factor[...]
    divisor = 0.8 * travel + 0.5
    numer_new = 0.5 - 0.2 * travel
    numer_old = 0.5 + 0.2 * travel
    ratio = numer_old / numer_new
    side = 1.0 / divisor
    table[0] = (0.8 * travel - 0.5) / divisor + ratio
    table[1] = ratio
    table[2] = numer_new / divisor
    table[3] = numer_old / divisor
    table[4] = side
    table[5] = factor[...] / (divisor * divisor)
    inner[...] = jnp.zeros(inner.shape, F32)
    leaving[...] = jnp.zeros(leaving.shape, F32)

    def eight(ref, g):
        return ref[pl.ds(pl.multiple_of(g * GROUP, GROUP), GROUP), :]

    def solve(g, carried):
        matrix_copy(g).wait()
        wide_copy(cot_hbm, cot, cot_sem, g).wait()
        lanes = [pl.ds(pl.multiple_of(g * WIDE + j * LANES, LANES), LANES) for j in range(GROUP)]
        carry, ratio, weight_new, weight_old = (eight(table.at[k], g) for k in range(4))
        exit_rows = eight(exits, g)
        opened = jnp.where(exit_rows >= 0, 1.0, 0.0)
        numbered = jnp.where(exit_rows >= 0, exit_rows + 1, 0).astype(F32)
        weights, twice, whole = [], [], []
        slots = []
        for j in range(GROUP):
            block = matrix[g * GROUP + j]
            weights.append(split(block))
            twice.append(jnp.concatenate([weights[-1][0]] * 2, 0))
            whole.append(jnp.concatenate(weights[-1], 0))
            pattern = jnp.where(block != 0.0, 1.0, 0.0).astype(BF16)
            slots.append(dot(jnp.broadcast_to(numbered[j : j + 1], (8, LANES)).astype(BF16), pattern)[0:1])
        adjoint = [None] * GROUP
        found = [[None] * steps for _ in range(GROUP)]
        gains = [[] for _ in range(GROUP)]
        for t in reversed(range(steps)):
            for j in range(GROUP):
                high, low = weights[j]
                start = cot[t, :, lanes[j]].astype(F32)
                if t == steps - 1:
                    x = jnp.concatenate([start, jnp.broadcast_to(opened[j : j + 1], (8, LANES))], 0).astype(BF16)
                    value = dot(jnp.concatenate([x, x], 1), whole[j])
                else:
                    x = jnp.concatenate([start, jnp.zeros((8, LANES), F32)], 0) + adjoint[j] * carry[j : j + 1]
                    x_high, x_low = split(x)
                    value = dot(jnp.concatenate([x_high, x_low], 1), twice[j]) + dot(x_high, low) - adjoint[j] * ratio[j : j + 1]
                adjoint[j] = value
                found[j][t] = value[:members]
                local[t, :, lanes[j]] = value[:members]
                gains[j].append(value[members : members + 1])
        total = inner[...]
        for j in range(GROUP):
            facts = rows_of(gains[j] + [slots[j], weight_new[j : j + 1], weight_old[j : j + 1]])
            gain[:, lanes[j]] = facts
            value = gather(jnp.concatenate(found[j] + [facts], 0), lax.rem(inlet[...], LANES))
            total = jnp.where(inlet[...] // LANES == g * GROUP + j, value, total)
        inner[...] = total
        return carried

    lax.fori_loop(0, groups, solve, 0)

    inside = inner[...]
    facts = inside[rows:]
    inside = inside[:rows]
    weight_new, weight_old = facts[5:6], facts[6:7]
    edge[...] = weight_new * inside + weight_old * jnp.concatenate(
        [inside[members:], jnp.zeros((members, LANES), F32)], 0
    )
    passed = [weight_new * facts[0:1]] + [weight_new * facts[d : d + 1] + weight_old * facts[d - 1 : d] for d in range(1, steps)]
    message = rows_of(passed + [facts[4:5]])
    for k in range(net):
        out_box[k, 0:8, :] = edge[pl.ds(k, 8, stride=stride), :]
        out_box[k, 8:16, :] = message
    in_box[me] = out_box[me]

    def outward(peer, slot):
        return pltpu.make_async_remote_copy(
            src_ref=out_box.at[peer, 0 : 8 + levels], dst_ref=in_box.at[slot, 0 : 8 + levels], send_sem=send.at[peer], recv_sem=recv.at[slot],
            device_id={"net": peer}, device_id_type=MESH,
        )

    def homeward(peer, slot):
        return pltpu.make_async_remote_copy(
            src_ref=back_box.at[peer], dst_ref=home_box.at[slot], send_sem=back_send.at[peer],
            recv_sem=back_recv.at[slot], device_id={"net": peer}, device_id_type=MESH,
        )

    def across(peer):
        return pltpu.make_async_remote_copy(
            src_ref=passing, dst_ref=arrived, send_sem=cross_sem.at[0], recv_sem=cross_sem.at[1],
            device_id={"net": peer}, device_id_type=MESH,
        )

    def sums(peer, slot):
        return pltpu.make_async_remote_copy(
            src_ref=sum_out.at[peer], dst_ref=sum_in.at[slot], send_sem=sum_send.at[peer], recv_sem=sum_recv.at[slot],
            device_id={"mem": peer}, device_id_type=MESH,
        )

    if net + mem > 2:
        pl.semaphore_wait(barrier, net + mem - 2)

    @pl.when(me > 0)
    def _():
        for i in far[:-1]:
            outward(peer_at(i), me).start()

    smalls[4].wait()

    def inflows(g, carried):
        wide_copy(flow_hbm, flow, flow_sem, g).wait()
        wide_copy(lateral_hbm, lateral, lateral_sem, g).wait()
        down_rows, exit_rows = eight(down, g), eight(exits, g)
        marks, out = [], []
        for j in range(GROUP):
            lanes = pl.ds(pl.multiple_of(g * WIDE + j * LANES, LANES), LANES)
            here = flow[:, :, lanes]
            flat = here.reshape(levels * members, LANES)
            inflow = dot_t(flat, one_hot(down_rows[j : j + 1], 0)).reshape(levels, members, LANES)
            marks.append(one_hot(exit_rows[j : j + 1], 0))
            facts = gain[:, lanes]
            held = here[:steps].astype(F32) - lateral[:, :, lanes].astype(F32)
            terms = 0.8 * held - 0.5 * inflow[1:] - 0.3 * inflow[:steps]
            out.append(jnp.sum(jnp.sum(terms * local[:, :, lanes], axis=0), axis=0, keepdims=True))
            for t in range(steps):
                weighted = terms[t] * facts[0:1]
                for d in range(1, t + 1):
                    weighted = weighted + terms[t - d] * facts[d : d + 1]
                term[t, :, lanes] = weighted
        partial[pl.ds(pl.multiple_of(g * GROUP, GROUP), GROUP), :] = rows_of(out)
        flat = flow[:, :, lanes_of(g)].reshape(levels * members, WIDE)
        leaving[...] += dot_t(flat, jnp.concatenate(marks, 1))
        return carried

    lax.fori_loop(0, groups, inflows, 0)

    crossed = leaving[...]
    passing[...] = -0.5 * crossed[members:] - 0.3 * crossed[:rows]

    for p in range(1, net):

        @pl.when(me != p)
        def _():
            outward(p, p).wait_recv()

    place = lax.broadcasted_iota(jnp.int32, (8, LANES), 0)
    state = in_box[net - 1, 0:8, :]
    back_box[net - 2] = state
    for p in reversed(range(1, net - 1)):
        slot = jnp.maximum(in_box[p, 12:13, :].astype(jnp.int32) - 1, 0)
        both = gather(state, slot)
        state = in_box[p, 0:8, :] + both * in_box[p, 8:9, :]
        for d in range(1, steps):
            passed = jnp.where(place < 8 - 2 * d, in_box[p, 8 + d : 9 + d, :], 0.0)
            state = state + pltpu.roll(both, 8 - 2 * d, 0) * passed
        back_box[p - 1] = state

    home_box[me] = back_box[me]
    for i in far[:-1]:
        peer = peer_at(i)

        @pl.when(peer < net - 1)
        def _():
            homeward(peer, me).start()

    @pl.when(me < net - 1)
    def _():
        across(me + 1).start()

    @pl.when(me == net - 1)
    def _():
        outer[...] = jnp.zeros(outer.shape, F32)

    @pl.when(me < net - 1)
    def _():
        for k in range(net):

            @pl.when(me != k)
            def _():
                homeward(k, k).wait_recv()

            outer[pl.ds(k, 8, stride=stride), :] = home_box[k]

    def taken_at(slot):
        return gather(outer[...], jnp.maximum(slot.astype(jnp.int32) - 1, 0))

    def weigh(g, carried):
        out = []
        for j in range(GROUP):
            lanes = pl.ds(pl.multiple_of(g * WIDE + j * LANES, LANES), LANES)
            value = taken_at(gain[4:5, lanes]).reshape(steps, members, LANES)
            taken[:, :, lanes] = value
            out.append(jnp.sum(jnp.sum(value * term[:, :, lanes], axis=0), axis=0, keepdims=True))
        here = pl.ds(pl.multiple_of(g * GROUP, GROUP), GROUP)
        partial[here, :] += rows_of(out)
        return carried

    lax.fori_loop(0, groups, weigh, 0)

    @pl.when(me > 0)
    def _():
        across(me).wait_recv()

    @pl.when(me == 0)
    def _():
        arrived[...] = jnp.zeros(arrived.shape, F32)

    came = arrived[...].reshape(steps, members, LANES)
    boundary = jnp.sum(came * inside.reshape(steps, members, LANES), axis=0)
    crossing = []
    for t in range(steps):
        weighted = came[t] * facts[0:1]
        for d in range(1, t + 1):
            weighted = weighted + came[t - d] * facts[d : d + 1]
        crossing.append(weighted)
    crossing = jnp.concatenate(crossing, 0)

    total = jnp.sum(taken_at(facts[4:5]) * crossing, axis=0, keepdims=True) + jnp.sum(boundary, axis=0, keepdims=True)
    size = partial.shape[0] // mem
    for k in range(mem):
        sum_out[k, 0:size, :] = partial[k * size : (k + 1) * size, :]
        sum_out[k, size : size + 1, :] = total
        sum_out[k, size + 1 :, :] = jnp.zeros((sum_out.shape[1] - size - 1, LANES), F32)
    sum_in[you] = sum_out[you]
    for i in near:
        sums(mate_at(i), you).start()

    def finish(g, carried):
        side = eight(table.at[4], g)
        for j in range(GROUP):
            lanes = pl.ds(pl.multiple_of(g * WIDE + j * LANES, LANES), LANES)
            facts = gain[:, lanes]
            value = taken[:, :, lanes]
            for t in range(steps):
                adjoint = local[t, :, lanes]
                for d in range(steps - t):
                    adjoint = adjoint + facts[d : d + 1] * value[t + d]
                grad[t, :, lanes] = (side[j : j + 1] * adjoint).astype(BF16)
        return carried

    lax.fori_loop(0, groups, finish, 0)

    for i in range(1, mem):
        peer = lax.rem(you + i, mem)
        sums(peer, peer).wait_recv()
    total = sum_in[0]
    for k in range(1, mem):
        total = total + sum_in[k]
    edge_row = total[size : size + 1]
    edge_high = edge_row.astype(BF16).astype(F32)
    edge_row = rows_of([edge_high, edge_row - edge_high]).astype(BF16)
    for i in range(size):
        block = you * size + i
        placed = dot_t(edge_row, one_hot(inlet[...], block * LANES))
        rough_out[i : i + 1, :] = (total[i : i + 1] + placed[0:1] + placed[1:2]) * table[5, pl.ds(block, 1), :]

    for i in range(1, mem):
        sums(lax.rem(you + i, mem), you).wait_send()

    @pl.when(me > 0)
    def _():
        for i in far[:-1]:
            outward(peer_at(i), me).wait_send()

    @pl.when(me < net - 1)
    def _():
        across(me + 1).wait_send()

    for i in far[:-1]:
        peer = peer_at(i)

        @pl.when(peer < net - 1)
        def _():
            homeward(peer, me).wait_send()


def store_kernel(grad, rough, grad_out, rough_out, sem):
    copies = [
        pltpu.make_async_copy(grad, grad_out, sem.at[0]),
        pltpu.make_async_copy(rough, rough_out, sem.at[1]),
    ]
    for copy in copies:
        copy.start()
    for copy in copies:
        copy.wait()


def body(stored_reach_flows, lateral, cotangent, roughness, travel_factor, inverse_block_matrix, down_in_block, exit_slot, inlet_reach):
    steps, members, reaches = cotangent.shape
    levels = steps + 1
    blocks = reaches // LANES
    groups = reaches // WIDE
    net, mem = lax.axis_size("net"), lax.axis_size("mem")

    def blocked(value):
        return value.reshape(blocks, LANES)

    anywhere = pl.BlockSpec(memory_space=pltpu.HBM)
    vmem = pl.BlockSpec(memory_space=pltpu.VMEM)
    dma = pltpu.SemaphoreType.DMA
    shaped = pltpu.VMEM
    per_block = [shaped((blocks, LANES), F32)] * 2 + [shaped((blocks, LANES), jnp.int32)]
    grad_lateral, grad_rough = pl.pallas_call(
        kernel,
        in_specs=[anywhere] * 9,
        out_specs=[vmem, vmem],
        out_shape=[
            pltpu.VMEM((steps, members, reaches), BF16),
            pltpu.VMEM((blocks // mem, LANES), F32),
        ],
        scratch_shapes=[
            shaped((steps, members, reaches), BF16),
            shaped((levels, members, reaches), BF16),
            shaped((steps, members, reaches), BF16),
            shaped((blocks, LANES, LANES), F32),
            *per_block,
            shaped((blocks, LANES), jnp.int32),
            shaped((1, LANES), jnp.int32),
            shaped((6, blocks, LANES), F32),
            shaped((steps, members, reaches), F32),
            shaped((8, reaches), F32),
            shaped((steps, members, reaches), F32),
            shaped((steps, members, reaches), F32),
            shaped((steps * members + 8, LANES), F32),
            shaped((levels * members, LANES), F32),
            shaped((steps * members, LANES), F32),
            shaped((steps * members, LANES), F32),
            shaped((steps * members, LANES), F32),
            shaped((steps * members, LANES), F32),
            shaped((net, 16, LANES), F32),
            shaped((net, 16, LANES), F32),
            shaped((net, 8, LANES), F32),
            shaped((net, 8, LANES), F32),
            shaped((blocks, LANES), F32),
            shaped((mem, 4, LANES), F32),
            shaped((mem, 4, LANES), F32),
            dma((5,)), dma((groups,)), dma((groups,)), dma((groups,)), dma((groups,)),
            dma((net,)), dma((net,)), dma((net,)), dma((net,)), dma((2,)), dma((mem,)), dma((mem,)),
        ],
        compiler_params=pltpu.CompilerParams(collective_id=0, has_side_effects=True, vmem_limit_bytes=56 << 20),
        name="adjoint",
    )(
        cotangent, stored_reach_flows, lateral, inverse_block_matrix, blocked(roughness), blocked(travel_factor),
        blocked(exit_slot), blocked(down_in_block), inlet_reach,
    )
    grad_lateral, grad_rough = pl.pallas_call(
        store_kernel,
        in_specs=[vmem, vmem],
        out_specs=[anywhere, anywhere],
        out_shape=[
            jax.ShapeDtypeStruct(grad_lateral.shape, BF16),
            jax.ShapeDtypeStruct(grad_rough.shape, F32),
        ],
        scratch_shapes=[dma((2,))],
        compiler_params=pltpu.CompilerParams(vmem_limit_bytes=4 << 20),
        name="store",
    )(grad_lateral, grad_rough)
    return grad_lateral, grad_rough.reshape(reaches // mem)


def solution(mesh):
    in_specs = (
        P(None, "mem", "net"),
        P(None, "mem", "net"),
        P(None, "mem", "net"),
        P("net"),
        P("net"),
        P("net", None, None),
        P("net"),
        P("net"),
        P("net", None),
    )
    out_specs = (P(None, "mem", "net"), P(("net", "mem")))
    return jax.shard_map(body, mesh=mesh, in_specs=in_specs, out_specs=out_specs, check_vma=False)
```

```python
import jax
import jax.numpy as jnp
from jax import lax
from jax.experimental import pallas as pl
from jax.experimental.pallas import tpu as pltpu
from jax.sharding import PartitionSpec as P

F32, BF16 = jnp.float32, jnp.bfloat16
LANES = 128
GROUP = 16
WIDE = GROUP * LANES
MESH = pl.DeviceIdType.MESH


def dot(a, b):
    return lax.dot_general(a, b, (((1,), (0,)), ((), ())), preferred_element_type=F32)


def dot_t(a, b):
    return lax.dot_general(a, b, (((1,), (1,)), ((), ())), preferred_element_type=F32)


def split(value):
    high = value.astype(BF16)
    return high, (value - high.astype(F32)).astype(BF16)


def stack_split(value):
    high = value.astype(BF16).astype(F32)
    return jnp.concatenate([high, value - high], 0).astype(BF16)


def halves(value):
    rows = value.shape[0] // 2
    return value[:rows] + value[rows:]


def rows_of(rows):
    if len(rows) > 8:
        return jnp.concatenate([rows_of(rows[:8]), rows_of(rows[8:])], 0)
    place = lax.broadcasted_iota(jnp.int32, (8, LANES), 0)
    out = jnp.zeros((8, LANES), F32)
    for i, row in enumerate(rows):
        out = jnp.where(place == i, jnp.broadcast_to(row, (8, LANES)), out)
    return out


def one_hot(row, start):
    place = lax.broadcasted_iota(jnp.int32, (LANES, LANES), 0) + start
    return jnp.where(place == row, 1.0, 0.0).astype(BF16)


def gather(value, row):
    return jnp.take_along_axis(value, jnp.broadcast_to(row, value.shape), axis=1, mode="promise_in_bounds")


def kernel(
    cot_hbm, flow_hbm, lateral_hbm, matrix_hbm, rough_hbm, factor_hbm, exits_hbm, down_hbm, inlet_hbm,
    grad, rough_out,
    cot, flow, lateral, matrix, rough, factor, exits, down, inlet,
    table, local, gain, term, taken, inner, leaving, passing, arrived, edge, outer,
    out_box, in_box, back_box, home_box, partial, sum_out, sum_in,
    small_sem, matrix_sem, cot_sem, flow_sem, lateral_sem,
    send, recv, back_send, back_recv, cross_sem, sum_send, sum_recv,
):
    net, mem = in_box.shape[0], sum_out.shape[0]
    spots = out_box.shape[0]
    lines = home_box.shape[1]
    steps, members, reaches = cot.shape
    levels = steps + 1
    rows = steps * members
    groups = reaches // WIDE
    me, you = lax.axis_index("net"), lax.axis_index("mem")

    near = sorted(range(1, mem), key=lambda i: -(i // 8 + min(i % 8 // 2, 4 - i % 8 // 2)))

    def mate_at(i):
        y = lax.rem(lax.rem(you // 2, 4) + i % 8 // 2, 4)
        return lax.rem(you // 8 + i // 8, 2) * 8 + y * 2 + lax.rem(lax.rem(you, 2) + i % 2, 2)

    far = sorted(range(net), key=lambda i: -(2 * (i % 2) + min(i // 2, spots - i // 2)))
    far_home = [i for i in far if i % 2 == 0]
    high, low = me // 2, lax.rem(me, 2)

    def peer_at(i):
        return 2 * lax.rem(high + i // 2, spots) + lax.rem(low + i % 2, 2)

    barrier = pltpu.get_barrier_semaphore()
    for i in far[:-1]:
        pl.semaphore_signal(barrier, inc=1, device_id={"net": peer_at(i)}, device_id_type=MESH)

    smalls = [
        pltpu.make_async_copy(a, b, small_sem.at[i])
        for i, (a, b) in enumerate(
            [(rough_hbm, rough), (factor_hbm, factor), (exits_hbm, exits), (inlet_hbm, inlet), (down_hbm, down)]
        )
    ]

    def lanes_of(g):
        return pl.ds(pl.multiple_of(g * WIDE, WIDE), WIDE)

    def matrix_copy(g):
        block = pl.ds(g * GROUP, GROUP)
        return pltpu.make_async_copy(matrix_hbm.at[block], matrix.at[block], matrix_sem.at[g])

    def wide_copy(source, target, sem, g):
        return pltpu.make_async_copy(source.at[:, :, lanes_of(g)], target.at[:, :, lanes_of(g)], sem.at[g])

    for copy in smalls[:4]:
        copy.start()
    for g in range(groups):
        matrix_copy(g).start()
        wide_copy(cot_hbm, cot, cot_sem, g).start()
    for i in near:
        pl.semaphore_signal(barrier, inc=1, device_id={"mem": mate_at(i)}, device_id_type=MESH)
    smalls[4].start()
    for g in range(groups):
        wide_copy(flow_hbm, flow, flow_sem, g).start()
        wide_copy(lateral_hbm, lateral, lateral_sem, g).start()

    for copy in smalls[:4]:
        copy.wait()
    travel = rough[...] * factor[...]
    divisor = 0.8 * travel + 0.5
    numer_new = 0.5 - 0.2 * travel
    numer_old = 0.5 + 0.2 * travel
    ratio = numer_old / numer_new
    side = 1.0 / divisor
    table[0] = (0.8 * travel - 0.5) / divisor + ratio
    table[1] = ratio
    table[2] = numer_new / divisor
    table[3] = numer_old / divisor
    table[4] = side
    table[5] = factor[...] / (divisor * divisor)
    inner[...] = jnp.zeros(inner.shape, F32)
    leaving[...] = jnp.zeros(leaving.shape, F32)

    def eight(ref, g):
        return ref[pl.ds(pl.multiple_of(g * GROUP, GROUP), GROUP), :]

    def solve(g, carried):
        matrix_copy(g).wait()
        wide_copy(cot_hbm, cot, cot_sem, g).wait()
        lanes = [pl.ds(pl.multiple_of(g * WIDE + j * LANES, LANES), LANES) for j in range(GROUP)]
        carry, ratio, weight_new, weight_old = (eight(table.at[k], g) for k in range(4))
        exit_rows = eight(exits, g)
        opened = jnp.where(exit_rows >= 0, 1.0, 0.0)
        numbered = jnp.where(exit_rows >= 0, exit_rows + 1, 0).astype(F32)
        weights, twice, whole = [], [], []
        slots = []
        for j in range(GROUP):
            block = matrix[g * GROUP + j]
            weights.append(split(block))
            twice.append(jnp.concatenate([weights[-1][0]] * 2, 0))
            whole.append(jnp.concatenate(weights[-1], 0))
            pattern = jnp.where(block != 0.0, 1.0, 0.0).astype(BF16)
            slots.append(dot(jnp.broadcast_to(numbered[j : j + 1], (8, LANES)).astype(BF16), pattern)[0:1])
        adjoint = [None] * GROUP
        found = [[None] * steps for _ in range(GROUP)]
        gains = [[] for _ in range(GROUP)]
        for t in reversed(range(steps)):
            for j in range(GROUP):
                high, low = weights[j]
                start = cot[t, :, lanes[j]].astype(F32)
                if t == steps - 1:
                    x = jnp.concatenate([start, jnp.broadcast_to(opened[j : j + 1], (8, LANES))], 0).astype(BF16)
                    value = dot(jnp.concatenate([x, x], 1), whole[j])
                else:
                    x = jnp.concatenate([start, jnp.zeros((8, LANES), F32)], 0) + adjoint[j] * carry[j : j + 1]
                    x_high, x_low = split(x)
                    value = dot(jnp.concatenate([x_high, x_low], 1), twice[j]) + dot(x_high, low) - adjoint[j] * ratio[j : j + 1]
                adjoint[j] = value
                found[j][t] = value[:members]
                local[t, :, lanes[j]] = value[:members]
                gains[j].append(value[members : members + 1])
        total = inner[...]
        for j in range(GROUP):
            facts = rows_of(gains[j] + [slots[j], weight_new[j : j + 1], weight_old[j : j + 1]])
            gain[:, lanes[j]] = facts
            value = gather(jnp.concatenate(found[j] + [facts], 0), lax.rem(inlet[...], LANES))
            total = jnp.where(inlet[...] // LANES == g * GROUP + j, value, total)
        inner[...] = total
        return carried

    lax.fori_loop(0, groups, solve, 0)

    inside = inner[...]
    facts = inside[rows:]
    inside = inside[:rows]
    weight_new, weight_old = facts[5:6], facts[6:7]
    edge[...] = weight_new * inside + weight_old * jnp.concatenate(
        [inside[members:], jnp.zeros((members, LANES), F32)], 0
    )
    passed = [weight_new * facts[0:1]] + [weight_new * facts[d : d + 1] + weight_old * facts[d - 1 : d] for d in range(1, steps)]
    message = rows_of(passed + [facts[4:5]])
    for k in range(spots):
        out_box[k, 0:lines, :] = edge[pl.ds(k, lines, stride=spots), :]
        out_box[k, lines : lines + 8, :] = message
    in_box[me] = out_box[high]

    def outward(peer, slot):
        return pltpu.make_async_remote_copy(
            src_ref=out_box.at[peer // 2, 0 : lines + levels], dst_ref=in_box.at[slot, 0 : lines + levels], send_sem=send.at[peer], recv_sem=recv.at[slot],
            device_id={"net": peer}, device_id_type=MESH,
        )

    def homeward(peer, slot):
        return pltpu.make_async_remote_copy(
            src_ref=back_box.at[peer], dst_ref=home_box.at[slot // 2], send_sem=back_send.at[peer],
            recv_sem=back_recv.at[slot // 2], device_id={"net": peer}, device_id_type=MESH,
        )

    def across(peer):
        return pltpu.make_async_remote_copy(
            src_ref=passing, dst_ref=arrived, send_sem=cross_sem.at[0], recv_sem=cross_sem.at[1],
            device_id={"net": peer}, device_id_type=MESH,
        )

    def sums(peer, slot):
        return pltpu.make_async_remote_copy(
            src_ref=sum_out.at[peer], dst_ref=sum_in.at[slot], send_sem=sum_send.at[peer], recv_sem=sum_recv.at[slot],
            device_id={"mem": peer}, device_id_type=MESH,
        )

    if net + mem > 2:
        pl.semaphore_wait(barrier, net + mem - 2)

    @pl.when(me > 0)
    def _():
        for i in far[:-1]:
            outward(peer_at(i), me).start()

    smalls[4].wait()

    def inflows(g, carried):
        wide_copy(flow_hbm, flow, flow_sem, g).wait()
        wide_copy(lateral_hbm, lateral, lateral_sem, g).wait()
        down_rows, exit_rows = eight(down, g), eight(exits, g)
        marks, out = [], []
        for j in range(GROUP):
            lanes = pl.ds(pl.multiple_of(g * WIDE + j * LANES, LANES), LANES)
            here = flow[:, :, lanes]
            flat = here.reshape(levels * members, LANES)
            inflow = dot_t(flat, one_hot(down_rows[j : j + 1], 0)).reshape(levels, members, LANES)
            marks.append(one_hot(exit_rows[j : j + 1], 0))
            facts = gain[:, lanes]
            held = here[:steps].astype(F32) - lateral[:, :, lanes].astype(F32)
            terms = 0.8 * held - 0.5 * inflow[1:] - 0.3 * inflow[:steps]
            out.append(jnp.sum(jnp.sum(terms * local[:, :, lanes], axis=0), axis=0, keepdims=True))
            for t in range(steps):
                weighted = terms[t] * facts[0:1]
                for d in range(1, t + 1):
                    weighted = weighted + terms[t - d] * facts[d : d + 1]
                term[t, :, lanes] = weighted
        partial[pl.ds(pl.multiple_of(g * GROUP, GROUP), GROUP), :] = rows_of(out)
        flat = flow[:, :, lanes_of(g)].reshape(levels * members, WIDE)
        leaving[...] += dot_t(flat, jnp.concatenate(marks, 1))
        return carried

    lax.fori_loop(0, groups, inflows, 0)

    crossed = leaving[...]
    passing[...] = -0.5 * crossed[members:] - 0.3 * crossed[:rows]

    for p in range(1, net):

        @pl.when(me != p)
        def _():
            outward(p, p).wait_recv()

    later = lines // steps
    place = lax.broadcasted_iota(jnp.int32, (lines, LANES), 0)
    state = in_box[net - 1, 0:lines, :]
    back_box[net - 2] = state
    for p in reversed(range(1, net - 1)):
        slot = jnp.maximum(in_box[p, lines + steps : lines + levels, :].astype(jnp.int32) - 1, 0)
        both = gather(state, slot)
        state = in_box[p, 0:lines, :] + both * in_box[p, lines : lines + 1, :]
        for d in range(1, steps):
            passed = jnp.where(place < lines - later * d, in_box[p, lines + d : lines + d + 1, :], 0.0)
            state = state + pltpu.roll(both, lines - later * d, 0) * passed
        back_box[p - 1] = state

    home_box[high] = back_box[me]
    for i in far_home[:-1]:
        peer = peer_at(i)

        @pl.when(peer < net - 1)
        def _():
            homeward(peer, me).start()

    @pl.when(me < net - 1)
    def _():
        across(me + 1).start()

    @pl.when(me > 0)
    def _():
        across(me).wait_recv()

    @pl.when(me == 0)
    def _():
        arrived[...] = jnp.zeros(arrived.shape, F32)

    came = arrived[...].reshape(steps, members, LANES)
    boundary = jnp.sum(came * inside.reshape(steps, members, LANES), axis=0)
    crossing = []
    for t in range(steps):
        weighted = came[t] * facts[0:1]
        for d in range(1, t + 1):
            weighted = weighted + came[t - d] * facts[d : d + 1]
        crossing.append(weighted)
    crossing = jnp.concatenate(crossing, 0)

    @pl.when(me == net - 1)
    def _():
        outer[...] = jnp.zeros(outer.shape, F32)

    @pl.when(me < net - 1)
    def _():
        for k in range(spots):

            @pl.when(high != k)
            def _():
                homeward(2 * k, 2 * k).wait_recv()

            outer[pl.ds(k, lines, stride=spots), :] = home_box[k]

    def taken_at(slot):
        return gather(outer[...], jnp.maximum(slot.astype(jnp.int32) - 1, 0))

    def weigh(g, carried):
        out = []
        for j in range(GROUP):
            lanes = pl.ds(pl.multiple_of(g * WIDE + j * LANES, LANES), LANES)
            value = taken_at(gain[4:5, lanes]).reshape(steps, members, LANES)
            taken[:, :, lanes] = value
            out.append(jnp.sum(jnp.sum(value * term[:, :, lanes], axis=0), axis=0, keepdims=True))
        here = pl.ds(pl.multiple_of(g * GROUP, GROUP), GROUP)
        partial[here, :] += rows_of(out)
        return carried

    lax.fori_loop(0, groups, weigh, 0)

    total = jnp.sum(taken_at(facts[4:5]) * crossing, axis=0, keepdims=True) + jnp.sum(boundary, axis=0, keepdims=True)
    size = partial.shape[0] // mem
    for k in range(mem):
        sum_out[k, 0:size, :] = partial[k * size : (k + 1) * size, :]
        sum_out[k, size : size + 1, :] = total
        sum_out[k, size + 1 :, :] = jnp.zeros((sum_out.shape[1] - size - 1, LANES), F32)
    sum_in[you] = sum_out[you]
    for i in near:
        sums(mate_at(i), you).start()

    def finish(g, carried):
        side = eight(table.at[4], g)
        for j in range(GROUP):
            lanes = pl.ds(pl.multiple_of(g * WIDE + j * LANES, LANES), LANES)
            facts = gain[:, lanes]
            value = taken[:, :, lanes]
            for t in range(steps):
                adjoint = local[t, :, lanes]
                for d in range(steps - t):
                    adjoint = adjoint + facts[d : d + 1] * value[t + d]
                grad[t, :, lanes] = (side[j : j + 1] * adjoint).astype(BF16)
        return carried

    lax.fori_loop(0, groups, finish, 0)

    for i in range(1, mem):
        peer = lax.rem(you + i, mem)
        sums(peer, peer).wait_recv()
    total = sum_in[0]
    for k in range(1, mem):
        total = total + sum_in[k]
    edge_row = total[size : size + 1]
    edge_high = edge_row.astype(BF16).astype(F32)
    edge_row = rows_of([edge_high, edge_row - edge_high]).astype(BF16)
    for i in range(size):
        block = you * size + i
        placed = dot_t(edge_row, one_hot(inlet[...], block * LANES))
        rough_out[i : i + 1, :] = (total[i : i + 1] + placed[0:1] + placed[1:2]) * table[5, pl.ds(block, 1), :]

    for i in range(1, mem):
        sums(lax.rem(you + i, mem), you).wait_send()

    @pl.when(me > 0)
    def _():
        for i in far[:-1]:
            outward(peer_at(i), me).wait_send()

    @pl.when(me < net - 1)
    def _():
        across(me + 1).wait_send()

    for i in far_home[:-1]:
        peer = peer_at(i)

        @pl.when(peer < net - 1)
        def _():
            homeward(peer, me).wait_send()


def store_kernel(grad, rough, grad_out, rough_out, sem):
    copies = [pltpu.make_async_copy(rough, rough_out, sem.at[0])]
    pieces = sem.shape[0] - 1
    for i in range(pieces):
        part = (i // 2, slice(None), slice(i % 2 * (grad.shape[2] // 2), (i % 2 + 1) * (grad.shape[2] // 2)))
        copies.append(pltpu.make_async_copy(grad.at[part], grad_out.at[part], sem.at[i + 1]))
    for copy in copies:
        copy.start()
    for copy in copies:
        copy.wait()


def body(stored_reach_flows, lateral, cotangent, roughness, travel_factor, inverse_block_matrix, down_in_block, exit_slot, inlet_reach):
    steps, members, reaches = cotangent.shape
    levels = steps + 1
    blocks = reaches // LANES
    groups = reaches // WIDE
    net, mem = lax.axis_size("net"), lax.axis_size("mem")
    spots = net // 2
    lines = steps * members // spots

    def blocked(value):
        return value.reshape(blocks, LANES)

    anywhere = pl.BlockSpec(memory_space=pltpu.HBM)
    vmem = pl.BlockSpec(memory_space=pltpu.VMEM)
    dma = pltpu.SemaphoreType.DMA
    shaped = pltpu.VMEM
    per_block = [shaped((blocks, LANES), F32)] * 2 + [shaped((blocks, LANES), jnp.int32)]
    grad_lateral, grad_rough = pl.pallas_call(
        kernel,
        in_specs=[anywhere] * 9,
        out_specs=[vmem, vmem],
        out_shape=[
            pltpu.VMEM((steps, members, reaches), BF16),
            pltpu.VMEM((blocks // mem, LANES), F32),
        ],
        scratch_shapes=[
            shaped((steps, members, reaches), BF16),
            shaped((levels, members, reaches), BF16),
            shaped((steps, members, reaches), BF16),
            shaped((blocks, LANES, LANES), F32),
            *per_block,
            shaped((blocks, LANES), jnp.int32),
            shaped((1, LANES), jnp.int32),
            shaped((6, blocks, LANES), F32),
            shaped((steps, members, reaches), F32),
            shaped((8, reaches), F32),
            shaped((steps, members, reaches), F32),
            shaped((steps, members, reaches), F32),
            shaped((steps * members + 8, LANES), F32),
            shaped((levels * members, LANES), F32),
            shaped((steps * members, LANES), F32),
            shaped((steps * members, LANES), F32),
            shaped((steps * members, LANES), F32),
            shaped((steps * members, LANES), F32),
            shaped((spots, lines + 8, LANES), F32),
            shaped((net, lines + 8, LANES), F32),
            shaped((net, lines, LANES), F32),
            shaped((spots, lines, LANES), F32),
            shaped((blocks, LANES), F32),
            shaped((mem, 4, LANES), F32),
            shaped((mem, 4, LANES), F32),
            dma((5,)), dma((groups,)), dma((groups,)), dma((groups,)), dma((groups,)),
            dma((net,)), dma((net,)), dma((net,)), dma((net,)), dma((2,)), dma((mem,)), dma((mem,)),
        ],
        compiler_params=pltpu.CompilerParams(collective_id=0, has_side_effects=True, vmem_limit_bytes=56 << 20),
        name="adjoint",
    )(
        cotangent, stored_reach_flows, lateral, inverse_block_matrix, blocked(roughness), blocked(travel_factor),
        blocked(exit_slot), blocked(down_in_block), inlet_reach,
    )
    grad_lateral, grad_rough = pl.pallas_call(
        store_kernel,
        in_specs=[vmem, vmem],
        out_specs=[anywhere, anywhere],
        out_shape=[
            jax.ShapeDtypeStruct(grad_lateral.shape, BF16),
            jax.ShapeDtypeStruct(grad_rough.shape, F32),
        ],
        scratch_shapes=[dma((2 * steps + 1,))],
        compiler_params=pltpu.CompilerParams(vmem_limit_bytes=4 << 20),
        name="store",
    )(grad_lateral, grad_rough)
    return grad_lateral, grad_rough.reshape(reaches // mem)


def solution(mesh):
    in_specs = (
        P(None, "mem", "net"),
        P(None, "mem", "net"),
        P(None, "mem", "net"),
        P("net"),
        P("net"),
        P("net", None, None),
        P("net"),
        P("net"),
        P("net", None),
    )
    out_specs = (P(None, "mem", "net"), P(("net", "mem")))
    return jax.shard_map(body, mesh=mesh, in_specs=in_specs, out_specs=out_specs, check_vma=False)
```

```python
import jax
import jax.numpy as jnp
from jax import lax
from jax.experimental import pallas as pl
from jax.experimental.pallas import tpu as pltpu
from jax.sharding import PartitionSpec as P

F32, BF16 = jnp.float32, jnp.bfloat16
LANES = 128
GROUP = 32
WIDE = GROUP * LANES
MESH = pl.DeviceIdType.MESH


def dot(a, b):
    return lax.dot_general(a, b, (((1,), (0,)), ((), ())), preferred_element_type=F32)


def dot_t(a, b):
    return lax.dot_general(a, b, (((1,), (1,)), ((), ())), preferred_element_type=F32)


def split(value):
    high = value.astype(BF16)
    return high, (value - high.astype(F32)).astype(BF16)


def stack_split(value):
    high = value.astype(BF16).astype(F32)
    return jnp.concatenate([high, value - high], 0).astype(BF16)


def halves(value):
    rows = value.shape[0] // 2
    return value[:rows] + value[rows:]


def rows_of(rows):
    if len(rows) > 8:
        return jnp.concatenate([rows_of(rows[i : i + 8]) for i in range(0, len(rows), 8)], 0)
    place = lax.broadcasted_iota(jnp.int32, (8, LANES), 0)
    out = jnp.zeros((8, LANES), F32)
    for i, row in enumerate(rows):
        out = jnp.where(place == i, jnp.broadcast_to(row, (8, LANES)), out)
    return out


def one_hot(row, start):
    place = lax.broadcasted_iota(jnp.int32, (LANES, LANES), 0) + start
    return jnp.where(place == row, 1.0, 0.0).astype(BF16)


def gather(value, row):
    return jnp.take_along_axis(value, jnp.broadcast_to(row, value.shape), axis=1, mode="promise_in_bounds")


def kernel(
    cot_hbm, flow_hbm, lateral_hbm, matrix_hbm, rough_hbm, factor_hbm, exits_hbm, down_hbm, inlet_hbm,
    grad, rough_out,
    cot, flow, lateral, matrix, rough, factor, exits, down, inlet,
    table, local, gain, term, taken, inner, leaving, passing, arrived, edge, outer,
    out_box, in_box, back_box, home_box, partial, sum_out, sum_in,
    small_sem, matrix_sem, cot_sem, flow_sem, lateral_sem,
    send, recv, back_send, back_recv, cross_sem, sum_send, sum_recv,
):
    net, mem = in_box.shape[0], sum_out.shape[0]
    spots = out_box.shape[0]
    lines = home_box.shape[1]
    steps, members, reaches = cot.shape
    levels = steps + 1
    rows = steps * members
    groups = reaches // WIDE
    me, you = lax.axis_index("net"), lax.axis_index("mem")

    near = sorted(range(1, mem), key=lambda i: -(i // 8 + min(i % 8 // 2, 4 - i % 8 // 2)))

    def mate_at(i):
        y = lax.rem(lax.rem(you // 2, 4) + i % 8 // 2, 4)
        return lax.rem(you // 8 + i // 8, 2) * 8 + y * 2 + lax.rem(lax.rem(you, 2) + i % 2, 2)

    far = sorted(range(net), key=lambda i: -(2 * (i % 2) + min(i // 2, spots - i // 2)))
    far_home = [i for i in far if i % 2 == 0]
    high, low = me // 2, lax.rem(me, 2)

    def peer_at(i):
        return 2 * lax.rem(high + i // 2, spots) + lax.rem(low + i % 2, 2)

    barrier = pltpu.get_barrier_semaphore()
    for i in far[:-1]:
        pl.semaphore_signal(barrier, inc=1, device_id={"net": peer_at(i)}, device_id_type=MESH)

    smalls = [
        pltpu.make_async_copy(a, b, small_sem.at[i])
        for i, (a, b) in enumerate(
            [(rough_hbm, rough), (factor_hbm, factor), (exits_hbm, exits), (inlet_hbm, inlet), (down_hbm, down)]
        )
    ]

    def lanes_of(g):
        return pl.ds(pl.multiple_of(g * WIDE, WIDE), WIDE)

    def matrix_copy(g):
        block = pl.ds(g * GROUP, GROUP)
        return pltpu.make_async_copy(matrix_hbm.at[block], matrix.at[block], matrix_sem.at[g])

    def wide_copy(source, target, sem, g):
        return pltpu.make_async_copy(source.at[:, :, lanes_of(g)], target.at[:, :, lanes_of(g)], sem.at[g])

    for copy in smalls[:4]:
        copy.start()
    for g in range(groups):
        matrix_copy(g).start()
        wide_copy(cot_hbm, cot, cot_sem, g).start()
    for i in near:
        pl.semaphore_signal(barrier, inc=1, device_id={"mem": mate_at(i)}, device_id_type=MESH)
    smalls[4].start()
    for g in range(groups):
        wide_copy(flow_hbm, flow, flow_sem, g).start()
        wide_copy(lateral_hbm, lateral, lateral_sem, g).start()

    for copy in smalls[:4]:
        copy.wait()
    travel = rough[...] * factor[...]
    divisor = 0.8 * travel + 0.5
    numer_new = 0.5 - 0.2 * travel
    numer_old = 0.5 + 0.2 * travel
    ratio = numer_old / numer_new
    side = 1.0 / divisor
    table[0] = (0.8 * travel - 0.5) / divisor + ratio
    table[1] = ratio
    table[2] = numer_new / divisor
    table[3] = numer_old / divisor
    table[4] = side
    table[5] = factor[...] / (divisor * divisor)
    inner[...] = jnp.zeros(inner.shape, F32)
    leaving[...] = jnp.zeros(leaving.shape, F32)

    def eight(ref, g):
        return ref[pl.ds(pl.multiple_of(g * GROUP, GROUP), GROUP), :]

    def solve(g, carried):
        matrix_copy(g).wait()
        wide_copy(cot_hbm, cot, cot_sem, g).wait()
        lanes = [pl.ds(pl.multiple_of(g * WIDE + j * LANES, LANES), LANES) for j in range(GROUP)]
        carry, ratio, weight_new, weight_old = (eight(table.at[k], g) for k in range(4))
        exit_rows = eight(exits, g)
        opened = jnp.where(exit_rows >= 0, 1.0, 0.0)
        numbered = jnp.where(exit_rows >= 0, exit_rows + 1, 0).astype(F32)
        weights, twice, whole = [], [], []
        slots = []
        for j in range(GROUP):
            block = matrix[g * GROUP + j]
            weights.append(split(block))
            twice.append(jnp.concatenate([weights[-1][0]] * 2, 0))
            whole.append(jnp.concatenate(weights[-1], 0))
            pattern = jnp.where(block != 0.0, 1.0, 0.0).astype(BF16)
            slots.append(dot(jnp.broadcast_to(numbered[j : j + 1], (8, LANES)).astype(BF16), pattern)[0:1])
        adjoint = [None] * GROUP
        found = [[None] * steps for _ in range(GROUP)]
        gains = [[] for _ in range(GROUP)]
        for t in reversed(range(steps)):
            for j in range(GROUP):
                high, low = weights[j]
                start = cot[t, :, lanes[j]].astype(F32)
                if t == steps - 1:
                    x = jnp.concatenate([start, jnp.broadcast_to(opened[j : j + 1], (8, LANES))], 0).astype(BF16)
                    value = dot(jnp.concatenate([x, x], 1), whole[j])
                else:
                    x = jnp.concatenate([start, jnp.zeros((8, LANES), F32)], 0) + adjoint[j] * carry[j : j + 1]
                    x_high, x_low = split(x)
                    value = dot(jnp.concatenate([x_high, x_low], 1), twice[j]) + dot(x_high, low) - adjoint[j] * ratio[j : j + 1]
                adjoint[j] = value
                found[j][t] = value[:members]
                local[t, :, lanes[j]] = value[:members]
                gains[j].append(value[members : members + 1])
        total = inner[...]
        for j in range(GROUP):
            facts = rows_of(gains[j] + [slots[j], weight_new[j : j + 1], weight_old[j : j + 1]])
            gain[:, lanes[j]] = facts
            value = gather(jnp.concatenate(found[j] + [facts], 0), lax.rem(inlet[...], LANES))
            total = jnp.where(inlet[...] // LANES == g * GROUP + j, value, total)
        inner[...] = total
        return carried

    lax.fori_loop(0, groups, solve, 0)

    inside = inner[...]
    facts = inside[rows:]
    inside = inside[:rows]
    weight_new, weight_old = facts[5:6], facts[6:7]
    edge[...] = weight_new * inside + weight_old * jnp.concatenate(
        [inside[members:], jnp.zeros((members, LANES), F32)], 0
    )
    passed = [weight_new * facts[0:1]] + [weight_new * facts[d : d + 1] + weight_old * facts[d - 1 : d] for d in range(1, steps)]
    message = rows_of(passed + [facts[4:5]])
    for k in range(spots):
        out_box[k, 0:lines, :] = edge[pl.ds(k, lines, stride=spots), :]
        out_box[k, lines : lines + 8, :] = message
    in_box[me] = out_box[high]

    def outward(peer, slot):
        return pltpu.make_async_remote_copy(
            src_ref=out_box.at[peer // 2, 0 : lines + levels], dst_ref=in_box.at[slot, 0 : lines + levels], send_sem=send.at[peer], recv_sem=recv.at[slot],
            device_id={"net": peer}, device_id_type=MESH,
        )

    def homeward(peer, slot):
        return pltpu.make_async_remote_copy(
            src_ref=back_box.at[peer], dst_ref=home_box.at[slot // 2], send_sem=back_send.at[peer],
            recv_sem=back_recv.at[slot // 2], device_id={"net": peer}, device_id_type=MESH,
        )

    def across(peer):
        return pltpu.make_async_remote_copy(
            src_ref=passing, dst_ref=arrived, send_sem=cross_sem.at[0], recv_sem=cross_sem.at[1],
            device_id={"net": peer}, device_id_type=MESH,
        )

    def sums(peer, slot):
        return pltpu.make_async_remote_copy(
            src_ref=sum_out.at[peer], dst_ref=sum_in.at[slot], send_sem=sum_send.at[peer], recv_sem=sum_recv.at[slot],
            device_id={"mem": peer}, device_id_type=MESH,
        )

    if net + mem > 2:
        pl.semaphore_wait(barrier, net + mem - 2)

    @pl.when(me > 0)
    def _():
        for i in far[:-1]:
            outward(peer_at(i), me).start()

    smalls[4].wait()

    def inflows(g, carried):
        wide_copy(flow_hbm, flow, flow_sem, g).wait()
        wide_copy(lateral_hbm, lateral, lateral_sem, g).wait()
        down_rows, exit_rows = eight(down, g), eight(exits, g)
        marks, out = [], []
        for j in range(GROUP):
            lanes = pl.ds(pl.multiple_of(g * WIDE + j * LANES, LANES), LANES)
            here = flow[:, :, lanes]
            flat = here.reshape(levels * members, LANES)
            inflow = dot_t(flat, one_hot(down_rows[j : j + 1], 0)).reshape(levels, members, LANES)
            marks.append(one_hot(exit_rows[j : j + 1], 0))
            facts = gain[:, lanes]
            held = here[:steps].astype(F32) - lateral[:, :, lanes].astype(F32)
            terms = 0.8 * held - 0.5 * inflow[1:] - 0.3 * inflow[:steps]
            out.append(jnp.sum(jnp.sum(terms * local[:, :, lanes], axis=0), axis=0, keepdims=True))
            for t in range(steps):
                weighted = terms[t] * facts[0:1]
                for d in range(1, t + 1):
                    weighted = weighted + terms[t - d] * facts[d : d + 1]
                term[t, :, lanes] = weighted
        partial[pl.ds(pl.multiple_of(g * GROUP, GROUP), GROUP), :] = rows_of(out)
        flat = flow[:, :, lanes_of(g)].reshape(levels * members, WIDE)
        leaving[...] += dot_t(flat, jnp.concatenate(marks, 1))
        return carried

    lax.fori_loop(0, groups, inflows, 0)

    crossed = leaving[...]
    passing[...] = -0.5 * crossed[members:] - 0.3 * crossed[:rows]

    for p in range(1, net):

        @pl.when(me != p)
        def _():
            outward(p, p).wait_recv()

    later = lines // steps
    place = lax.broadcasted_iota(jnp.int32, (lines, LANES), 0)
    state = in_box[net - 1, 0:lines, :]
    back_box[net - 2] = state
    for p in reversed(range(1, net - 1)):
        slot = jnp.maximum(in_box[p, lines + steps : lines + levels, :].astype(jnp.int32) - 1, 0)
        both = gather(state, slot)
        state = in_box[p, 0:lines, :] + both * in_box[p, lines : lines + 1, :]
        for d in range(1, steps):
            passed = jnp.where(place < lines - later * d, in_box[p, lines + d : lines + d + 1, :], 0.0)
            state = state + pltpu.roll(both, lines - later * d, 0) * passed
        back_box[p - 1] = state

    home_box[high] = back_box[me]
    for i in far_home[:-1]:
        peer = peer_at(i)

        @pl.when(peer < net - 1)
        def _():
            homeward(peer, me).start()

    @pl.when(me < net - 1)
    def _():
        across(me + 1).start()

    @pl.when(me > 0)
    def _():
        across(me).wait_recv()

    @pl.when(me == 0)
    def _():
        arrived[...] = jnp.zeros(arrived.shape, F32)

    came = arrived[...].reshape(steps, members, LANES)
    boundary = jnp.sum(came * inside.reshape(steps, members, LANES), axis=0)
    crossing = []
    for t in range(steps):
        weighted = came[t] * facts[0:1]
        for d in range(1, t + 1):
            weighted = weighted + came[t - d] * facts[d : d + 1]
        crossing.append(weighted)
    crossing = jnp.concatenate(crossing, 0)

    @pl.when(me == net - 1)
    def _():
        outer[...] = jnp.zeros(outer.shape, F32)

    @pl.when(me < net - 1)
    def _():
        for k in range(spots):

            @pl.when(high != k)
            def _():
                homeward(2 * k, 2 * k).wait_recv()

            outer[pl.ds(k, lines, stride=spots), :] = home_box[k]

    def taken_at(slot):
        return gather(outer[...], jnp.maximum(slot.astype(jnp.int32) - 1, 0))

    def weigh(g, carried):
        out = []
        for j in range(GROUP):
            lanes = pl.ds(pl.multiple_of(g * WIDE + j * LANES, LANES), LANES)
            value = taken_at(gain[4:5, lanes]).reshape(steps, members, LANES)
            taken[:, :, lanes] = value
            out.append(jnp.sum(jnp.sum(value * term[:, :, lanes], axis=0), axis=0, keepdims=True))
        here = pl.ds(pl.multiple_of(g * GROUP, GROUP), GROUP)
        partial[here, :] += rows_of(out)
        return carried

    lax.fori_loop(0, groups, weigh, 0)

    total = jnp.sum(taken_at(facts[4:5]) * crossing, axis=0, keepdims=True) + jnp.sum(boundary, axis=0, keepdims=True)
    size = partial.shape[0] // mem
    for k in range(mem):
        sum_out[k, 0:size, :] = partial[k * size : (k + 1) * size, :]
        sum_out[k, size : size + 1, :] = total
        sum_out[k, size + 1 :, :] = jnp.zeros((sum_out.shape[1] - size - 1, LANES), F32)
    sum_in[you] = sum_out[you]
    for i in near:
        sums(mate_at(i), you).start()

    def finish(g, carried):
        side = eight(table.at[4], g)
        for j in range(GROUP):
            lanes = pl.ds(pl.multiple_of(g * WIDE + j * LANES, LANES), LANES)
            facts = gain[:, lanes]
            value = taken[:, :, lanes]
            for t in range(steps):
                adjoint = local[t, :, lanes]
                for d in range(steps - t):
                    adjoint = adjoint + facts[d : d + 1] * value[t + d]
                grad[t, :, lanes] = (side[j : j + 1] * adjoint).astype(BF16)
        return carried

    lax.fori_loop(0, groups, finish, 0)

    for i in range(1, mem):
        peer = lax.rem(you + i, mem)
        sums(peer, peer).wait_recv()
    total = sum_in[0]
    for k in range(1, mem):
        total = total + sum_in[k]
    edge_row = total[size : size + 1]
    edge_high = edge_row.astype(BF16).astype(F32)
    edge_row = rows_of([edge_high, edge_row - edge_high]).astype(BF16)
    for i in range(size):
        block = you * size + i
        placed = dot_t(edge_row, one_hot(inlet[...], block * LANES))
        rough_out[i : i + 1, :] = (total[i : i + 1] + placed[0:1] + placed[1:2]) * table[5, pl.ds(block, 1), :]

    for i in range(1, mem):
        sums(lax.rem(you + i, mem), you).wait_send()

    @pl.when(me > 0)
    def _():
        for i in far[:-1]:
            outward(peer_at(i), me).wait_send()

    @pl.when(me < net - 1)
    def _():
        across(me + 1).wait_send()

    for i in far_home[:-1]:
        peer = peer_at(i)

        @pl.when(peer < net - 1)
        def _():
            homeward(peer, me).wait_send()


def store_kernel(grad, rough, grad_out, rough_out, sem):
    copies = [pltpu.make_async_copy(rough, rough_out, sem.at[0])]
    pieces = sem.shape[0] - 1
    for i in range(pieces):
        part = (i // 2, slice(None), slice(i % 2 * (grad.shape[2] // 2), (i % 2 + 1) * (grad.shape[2] // 2)))
        copies.append(pltpu.make_async_copy(grad.at[part], grad_out.at[part], sem.at[i + 1]))
    for copy in copies:
        copy.start()
    for copy in copies:
        copy.wait()


def body(stored_reach_flows, lateral, cotangent, roughness, travel_factor, inverse_block_matrix, down_in_block, exit_slot, inlet_reach):
    steps, members, reaches = cotangent.shape
    levels = steps + 1
    blocks = reaches // LANES
    groups = reaches // WIDE
    net, mem = lax.axis_size("net"), lax.axis_size("mem")
    spots = net // 2
    lines = steps * members // spots

    def blocked(value):
        return value.reshape(blocks, LANES)

    anywhere = pl.BlockSpec(memory_space=pltpu.HBM)
    vmem = pl.BlockSpec(memory_space=pltpu.VMEM)
    dma = pltpu.SemaphoreType.DMA
    shaped = pltpu.VMEM
    per_block = [shaped((blocks, LANES), F32)] * 2 + [shaped((blocks, LANES), jnp.int32)]
    grad_lateral, grad_rough = pl.pallas_call(
        kernel,
        in_specs=[anywhere] * 9,
        out_specs=[vmem, vmem],
        out_shape=[
            pltpu.VMEM((steps, members, reaches), BF16),
            pltpu.VMEM((blocks // mem, LANES), F32),
        ],
        scratch_shapes=[
            shaped((steps, members, reaches), BF16),
            shaped((levels, members, reaches), BF16),
            shaped((steps, members, reaches), BF16),
            shaped((blocks, LANES, LANES), F32),
            *per_block,
            shaped((blocks, LANES), jnp.int32),
            shaped((1, LANES), jnp.int32),
            shaped((6, blocks, LANES), F32),
            shaped((steps, members, reaches), F32),
            shaped((8, reaches), F32),
            shaped((steps, members, reaches), F32),
            shaped((steps, members, reaches), F32),
            shaped((steps * members + 8, LANES), F32),
            shaped((levels * members, LANES), F32),
            shaped((steps * members, LANES), F32),
            shaped((steps * members, LANES), F32),
            shaped((steps * members, LANES), F32),
            shaped((steps * members, LANES), F32),
            shaped((spots, lines + 8, LANES), F32),
            shaped((net, lines + 8, LANES), F32),
            shaped((net, lines, LANES), F32),
            shaped((spots, lines, LANES), F32),
            shaped((blocks, LANES), F32),
            shaped((mem, 4, LANES), F32),
            shaped((mem, 4, LANES), F32),
            dma((5,)), dma((groups,)), dma((groups,)), dma((groups,)), dma((groups,)),
            dma((net,)), dma((net,)), dma((net,)), dma((net,)), dma((2,)), dma((mem,)), dma((mem,)),
        ],
        compiler_params=pltpu.CompilerParams(collective_id=0, has_side_effects=True, vmem_limit_bytes=56 << 20),
        name="adjoint",
    )(
        cotangent, stored_reach_flows, lateral, inverse_block_matrix, blocked(roughness), blocked(travel_factor),
        blocked(exit_slot), blocked(down_in_block), inlet_reach,
    )
    grad_lateral, grad_rough = pl.pallas_call(
        store_kernel,
        in_specs=[vmem, vmem],
        out_specs=[anywhere, anywhere],
        out_shape=[
            jax.ShapeDtypeStruct(grad_lateral.shape, BF16),
            jax.ShapeDtypeStruct(grad_rough.shape, F32),
        ],
        scratch_shapes=[dma((2 * steps + 1,))],
        compiler_params=pltpu.CompilerParams(vmem_limit_bytes=4 << 20),
        name="store",
    )(grad_lateral, grad_rough)
    return grad_lateral, grad_rough.reshape(reaches // mem)


def solution(mesh):
    in_specs = (
        P(None, "mem", "net"),
        P(None, "mem", "net"),
        P(None, "mem", "net"),
        P("net"),
        P("net"),
        P("net", None, None),
        P("net"),
        P("net"),
        P("net", None),
    )
    out_specs = (P(None, "mem", "net"), P(("net", "mem")))
    return jax.shard_map(body, mesh=mesh, in_specs=in_specs, out_specs=out_specs, check_vma=False)
```
